256 devices in a mesh: tok: 16 (over x_hi, y, core), ch: 16 (over z, x_lo).
Axes of the slice: x: 4 (x_hi: 2, x_lo: 2; x = x_hi * 2 + x_lo), y: 4, z: 8, core: 2. Of those that a mesh axis runs over, the one named last changes fastest.
Arguments:
- inputs: float32 [4096, 4096], P('tok', 'ch'), may hold values from -6 to 6
- grad_out: float32 [4096, 4096], P('tok', 'ch'), may hold values from -6 to 6
- blocks_one: float32 [16, 16, 4, 128, 128], P(None, 'ch'), may hold values from -0.1875 to 0.1875
- slots_one: int32 [16, 16, 4], P(None, 'ch'), may hold values from 0 to 128, as said below
- blocks_two: float32 [16, 16, 4, 128, 128], P(None, 'ch'), may hold values from -0.125 to 0.125
- slots_two: int32 [16, 16, 4], P(None, 'ch'), may hold values from 0 to 128, as said below
Outputs:
- grad_x: float32 [4096, 4096], P('tok', 'ch')
- grad_one: float32 [16, 16, 4, 128, 128], P('tok', 'ch')
- grad_two: float32 [16, 16, 4, 128, 128], P('tok', 'ch')
The draws below stay inside these ranges and needn't reach their ends.
Inputs may be any that keep to these rules, and one draw needn't show every extreme that they name: For each hidden shard j, the live entries of slots_one[:, j, :] (those under 128) are distinct block positions; 128 marks an empty entry, live entries stand first in each owner's list, and in every shard one owner has all 4 entries live. Likewise for slots_two: distinct live positions in each shard, 128 marks an empty entry, live entries first, one owner of each shard with all 4 entries live.
All inputs are finite; a program needn't handle non-finite values.
Results may differ from the reference program's by a relative error of at most 0.0003.
Values sent between devices are 32-bit elements; how exact they have to be, the bound alone decides.
A program may use at most 192 MiB of HBM per device.

```python
import math
from functools import partial
import jax
import jax.numpy as jnp
from jax import lax

D = 4096
H = 8192
BLK = 128
CAP = 4
OWNERS = 16
SHARDS = 16
HID_DEV = 512
SLOTS = 128
TOKENS = 4096


def owner_lists(key):

    def one_shard(shard_key):
        key_count, key_busy, key_order = jax.random.split(shard_key, 3)
        counts = jax.random.randint(key_count, (OWNERS,), 0, CAP + 1)
        busiest = jax.random.randint(key_busy, (), 0, OWNERS)
        counts = jnp.where(jnp.arange(OWNERS) == busiest, CAP, counts)
        slot_order = jax.random.permutation(key_order, SLOTS)
        starts = jnp.cumsum(counts) - counts
        places = starts[:, None] + jnp.arange(CAP)[None, :]
        is_live = jnp.arange(CAP)[None, :] < counts[:, None]
        chosen = slot_order[jnp.clip(places, 0, SLOTS - 1)]
        return jnp.where(is_live, chosen, SLOTS).astype(jnp.int32)
    shard_keys = jax.random.split(key, SHARDS)
    owner_table = jax.vmap(one_shard)(shard_keys)
    return jnp.transpose(owner_table, (1, 0, 2))


def draw_slots_one(key, part):
    return owner_lists(jax.random.fold_in(key, 11))


def draw_slots_two(key, part):
    return owner_lists(jax.random.fold_in(key, 23))


def level_of(rng, extent, shards, low, largest):
    loudness, own = 1.0, jax.random.fold_in(rng, 6)
    for axis_at, parts in shards:
        steps = jnp.exp(jax.random.uniform(jax.random.fold_in(own, axis_at), (parts,), jnp.float32, low / len(shards), largest / len(shards)))
        loudness = loudness * jnp.repeat(steps, extent[axis_at] // parts).reshape([-1 if axis == axis_at else 1 for axis in range(len(extent))])
    return loudness


def centred(own_key, extent, deviation, bound, cuts=(), kind=jnp.bfloat16):
    result = jax.random.normal(own_key, extent, jnp.float32) * deviation
    if len(cuts) > 0:
        result = level_of(own_key, extent, cuts, -0.22, 0.18) * result
    return jnp.clip(result, min=-bound, max=bound).astype(kind)


def setup_inputs(seed: int = 0) -> dict:
    key_of = jax.random.split(jax.random.key(seed), 7)
    inputs = centred(key_of[0], (TOKENS, D), 1.0, 6.0, ((0, 16), (1, 16)), jnp.float32)
    grad_out = centred(key_of[1], (TOKENS, D), 1.0, 6.0, ((0, 16), (1, 16)), jnp.float32)
    blocks_one = centred(key_of[2], (OWNERS, SHARDS, CAP, BLK, BLK), (D // 4) ** -0.5, 0.1875, ((1, 16),), jnp.float32)
    slots_one = draw_slots_one(jax.random.fold_in(key_of[6], 71), 0)
    blocks_two = centred(key_of[4], (OWNERS, SHARDS, CAP, BLK, BLK), (H // 4) ** -0.5, 0.125, ((1, 16),), jnp.float32)
    slots_two = draw_slots_two(jax.random.fold_in(key_of[6], 71), 0)
    return {"inputs": inputs, "grad_out": grad_out, "blocks_one": blocks_one, "slots_one": slots_one, "blocks_two": blocks_two, "slots_two": slots_two}


HIGH = lax.Precision.HIGHEST

def table_to_dense(block_table, first_dim, second_dim):
    block_size = block_table.shape[-1]
    grid = block_table.reshape(first_dim, second_dim, block_size, block_size).transpose(0, 2, 1, 3)
    return grid.reshape(first_dim * block_size, second_dim * block_size)

def dense_to_table(dense, first_dim, second_dim):
    block_size = dense.shape[0] // first_dim
    grid = dense.reshape(first_dim, block_size, second_dim, block_size).transpose(0, 2, 1, 3)
    return grid.reshape(first_dim * second_dim, block_size, block_size)

def rebuild(blocks, slot_ids, first_dim, second_dim):
    block_size = blocks.shape[-1]
    flat_blocks = blocks.reshape(-1, block_size, block_size)
    flat_ids = slot_ids.reshape(-1)
    empty = jnp.zeros((first_dim * second_dim, block_size, block_size), blocks.dtype)
    filled = empty.at[flat_ids].set(flat_blocks, mode='drop')
    return table_to_dense(filled, first_dim, second_dim)

def pick_blocks(block_table, slot_ids):
    return jnp.take(block_table, slot_ids, axis=0, mode='fill', fill_value=0.0)

def reference(inputs, grad_out, blocks_one, slots_one, blocks_two, slots_two):
    block_size = blocks_one.shape[-1]
    feat_blocks = D // block_size
    hid_blocks = HID_DEV // block_size
    make_one = jax.vmap(partial(rebuild, first_dim=feat_blocks, second_dim=hid_blocks), in_axes=(1, 1))
    make_two = jax.vmap(partial(rebuild, first_dim=hid_blocks, second_dim=feat_blocks), in_axes=(1, 1))
    dense_one = make_one(blocks_one, slots_one).transpose(1, 0, 2).reshape(D, H)
    dense_two = make_two(blocks_two, slots_two).reshape(H, D)
    pre_act = jnp.dot(inputs, dense_one, precision=HIGH)
    normal_cdf = 0.5 * (1.0 + lax.erf(pre_act * (1.0 / math.sqrt(2.0))))
    normal_pdf = jnp.exp(-0.5 * pre_act * pre_act) * (1.0 / math.sqrt(2.0 * math.pi))
    activated = pre_act * normal_cdf
    grad_act = jnp.dot(grad_out, dense_two.T, precision=HIGH)
    grad_pre = grad_act * (normal_cdf + pre_act * normal_pdf)
    grad_x = jnp.dot(grad_pre, dense_one.T, precision=HIGH)
    factor = 1.0 / math.sqrt(TOKENS)
    full_one = jnp.dot(inputs.T, grad_pre, precision=HIGH) * factor
    full_two = jnp.dot(activated.T, grad_out, precision=HIGH) * factor
    shard_one = full_one.reshape(D, SHARDS, HID_DEV).transpose(1, 0, 2)
    shard_two = full_two.reshape(SHARDS, HID_DEV, D)
    tables_one = jax.vmap(partial(dense_to_table, first_dim=feat_blocks, second_dim=hid_blocks))(shard_one)
    tables_two = jax.vmap(partial(dense_to_table, first_dim=hid_blocks, second_dim=feat_blocks))(shard_two)
    grad_one = jax.vmap(pick_blocks, in_axes=(0, 1), out_axes=1)(tables_one, slots_one)
    grad_two = jax.vmap(pick_blocks, in_axes=(0, 1), out_axes=1)(tables_two, slots_two)
    return (grad_x, grad_one, grad_two)
```

```python
import functools
import math

import jax
import jax.numpy as jnp
from jax import lax
from jax.experimental import pallas as pl
from jax.experimental.pallas import tpu as pltpu
from jax.sharding import PartitionSpec as P

F32 = jnp.float32
BF16 = jnp.bfloat16
MESH = pl.DeviceIdType.MESH
NZ, NXL, NXH, NY = 8, 2, 2, 4

SLOTS = [
    (0, 0),
    (0, -1), (0, 1), (1, 0),
    (0, -2), (0, 2), (1, 1),
    (0, -3), (0, 3), (1, -1),
    (0, 4), (1, -2), (1, 2),
    (1, -3), (1, 3), (1, 4),
]
SLOT = {key: at for at, key in enumerate(SLOTS)}
SLOT[(0, -4)] = SLOT[(0, 4)]
SLOT[(1, -4)] = SLOT[(1, 4)]
NT = (((1,), (1,)), ((), ()))
NN = (((1,), (0,)), ((), ()))

N_COPIES = 60 + 17 + 22


def dot(a, b, dims):
    return lax.dot_general(a, b, dims, preferred_element_type=F32)


def split(v):
    high = v.astype(BF16)
    return high, (v - high.astype(F32)).astype(BF16)


def kernel(
    tab, x_in, dy_in, w1_hbm, w2_hbm,
    gx_out, g1_out, g2_out,
    raw1, raw2, xg, dyg, w1h, w1l, w2h, w2l, table,
    sh, sl, pre, ga, slope, act_th, act_tl, gp_th, gp_tl, gph, gpl,
    gx, rs_buf, core_buf, y_buf, far_buf,
    send_sem, recv_sem, local_sem,
):
    t = lax.axis_index("tok")
    c = lax.axis_index("ch")
    core = lax.rem(t, 2)
    y = lax.rem(lax.div(t, 2), NY)
    xh = lax.div(t, 2 * NY)
    xl = lax.rem(c, 2)
    z = lax.div(c, 2)

    def at_z(step):
        return (t, lax.rem(z + step, NZ) * 2 + xl)

    def at_y(step):
        return ((xh * NY + lax.rem(y + step, NY)) * 2 + core, c)

    zp, zm = at_z(1), at_z(NZ - 1)
    yp, ym = at_y(1), at_y(NY - 1)
    xp = (t, z * 2 + (1 - xl))
    cp = ((xh * NY + y) * 2 + (1 - core), c)
    hp = (((1 - xh) * NY + y) * 2 + core, c)

    fetch1 = pltpu.make_async_copy(w1_hbm, raw1.at[pl.ds(0, 64)], local_sem.at[0])
    fetch2 = pltpu.make_async_copy(w2_hbm, raw2.at[pl.ds(0, 64)], local_sem.at[1])
    fetch1.start()
    fetch2.start()

    barrier = pltpu.get_barrier_semaphore()
    for peer in (zp, zm, xp, yp, ym, cp, hp):
        pl.semaphore_signal(barrier, inc=1, device_id=peer, device_id_type=MESH)
    pl.semaphore_wait(barrier, 7)

    copies = []

    def send(src, dst, peer):
        at = len(copies)
        copy = pltpu.make_async_remote_copy(
            src_ref=src, dst_ref=dst, send_sem=send_sem.at[at], recv_sem=recv_sem.at[at],
            device_id=peer, device_id_type=MESH,
        )
        copy.start()
        copies.append(copy)
        return copy

    rows = {"a": pl.ds(0, 128), "b": pl.ds(128, 128)}
    arrivals = {}

    def forward(phase, source, col, dz, half, link):
        peer = {"+": zp, "-": zm, "x": xp}[link]
        to = {"+": (col, dz - 1), "-": (col, dz + 1), "x": (1 - col, dz)}[link]
        buf = xg if phase == 0 else dyg
        src = source if (col, dz) == (0, 0) else buf.at[SLOT[(col, dz)]]
        copy = send(src.at[rows[half]], buf.at[SLOT[to], rows[half]], peer)
        arrivals[(phase, SLOT[to], half)] = copy

    def arrive(phase, key, halves="ab"):
        for half in halves:
            arrivals[(phase, SLOT[key], half)].wait_recv()

    def open_phase(phase, source):
        for half in "ab":
            for link in "+-x":
                forward(phase, source, 0, 0, half, link)

    def round_1(phase, source):
        for half in "ab":
            arrive(phase, (0, -1), half)
            forward(phase, source, 0, -1, half, "+")
            arrive(phase, (0, 1), half)
            forward(phase, source, 0, 1, half, "-")
            forward(phase, source, 0, 1, half, "x")
        for half in "ab":
            forward(phase, source, 0, -1, half, "x")
        arrive(phase, (1, 0))

    def round_2(phase, source):
        for half in "ab":
            arrive(phase, (0, -2), half)
            forward(phase, source, 0, -2, half, "+")
            arrive(phase, (0, 2), half)
            forward(phase, source, 0, 2, half, "-")
        arrive(phase, (1, 1))

    def round_3(phase, source):
        arrive(phase, (0, -3), "a")
        forward(phase, source, 0, -3, "a", "+")
        forward(phase, source, 0, -3, "a", "x")
        for half in "ab":
            forward(phase, source, 1, 1, half, "-")
        arrive(phase, (0, 3), "a")
        arrive(phase, (0, 3), "b")
        forward(phase, source, 0, 3, "b", "-")
        forward(phase, source, 0, 3, "b", "x")
        arrive(phase, (0, -3), "b")
        arrive(phase, (1, -1))
        for half in "ab":
            forward(phase, source, 1, -1, half, "+")
        forward(phase, source, 0, -3, "b", "x")
        forward(phase, source, 0, 3, "a", "x")

    def round_4(phase, source):
        arrive(phase, (0, 4))
        arrive(phase, (1, -3), "a")
        forward(phase, source, 1, -3, "a", "+")
        arrive(phase, (1, 3), "b")
        forward(phase, source, 1, 3, "b", "-")

    def round_5(phase):
        arrive(phase, (1, -2))
        arrive(phase, (1, 2))
        arrive(phase, (1, -3), "b")
        arrive(phase, (1, 3), "a")
        arrive(phase, (1, 4))

    def take_x(s, carry):
        for q in range(2):
            for h in range(4):
                high, low = split(raw1[tab[s * 8 + q * 4 + h]])
                w1h[s, pl.ds(q * 128, 128), pl.ds(h * 128, 128)] = high
                w1l[s, pl.ds(q * 128, 128), pl.ds(h * 128, 128)] = low
        high, low = split(xg[s])
        sh[...] = high
        sl[...] = low
        pre[...] += (
            dot(sh[...], w1h[s], NN) + dot(sh[...], w1l[s], NN) + dot(sl[...], w1h[s], NN)
        )
        return carry

    def to_table(s, th, tl):
        full = dot(th[...], sh[...], NN) + dot(th[...], sl[...], NN) + dot(tl[...], sh[...], NN)
        for q in range(2):
            for h in range(4):
                table[s * 8 + q * 4 + h] = full[h * 128 : h * 128 + 128, q * 128 : q * 128 + 128]

    def take_dy(s, carry):
        for q in range(2):
            for h in range(4):
                high, low = split(raw2[tab[128 + s * 8 + q * 4 + h]])
                w2h[pl.ds(h * 128, 128), pl.ds(q * 128, 128)] = high
                w2l[pl.ds(h * 128, 128), pl.ds(q * 128, 128)] = low
        high, low = split(dyg[s])
        sh[...] = high
        sl[...] = low
        ga[...] += (
            dot(sh[...], w2h[...], NT) + dot(sh[...], w2l[...], NT) + dot(sl[...], w2h[...], NT)
        )
        to_table(s, act_th, act_tl)
        return carry

    def take_w1(s, carry):
        high, low = split(xg[s])
        sh[...] = high
        sl[...] = low
        to_table(s, gp_th, gp_tl)
        return carry

    def grad_x(s, carry):
        gx[s] = dot(gph[...], w1h[s], NT) + dot(gph[...], w1l[s], NT) + dot(gpl[...], w1h[s], NT)
        return carry

    def run(body, first, last):
        lax.fori_loop(first, last, body, 0)

    def transposed(value, r, th, tl):
        high, low = split(value.T)
        th[:, r] = high
        tl[:, r] = low

    open_phase(0, x_in)
    xg[0] = x_in[...]
    pre[...] = jnp.zeros_like(pre)
    raw1[64] = jnp.zeros((128, 128), F32)
    fetch1.wait()
    run(take_x, 0, 1)
    round_1(0, x_in)
    run(take_x, 1, 4)
    round_2(0, x_in)
    run(take_x, 4, 7)
    round_3(0, x_in)
    run(take_x, 7, 10)
    dyg[0] = dy_in[...]
    ga[...] = jnp.zeros_like(ga)
    raw2[64] = jnp.zeros((128, 128), F32)
    table[128] = jnp.zeros((128, 128), F32)
    fetch2.wait()
    round_4(0, x_in)
    open_phase(1, dy_in)
    run(take_x, 10, 11)
    round_5(0)
    run(take_x, 11, 16)
    round_1(1, dy_in)
    for part in range(2):
        r = pl.ds(part * 128, 128)
        p = pre[r, :]
        cdf = 0.5 * (1.0 + lax.erf(p * (1.0 / math.sqrt(2.0))))
        pdf = jnp.exp(-0.5 * p * p) * (1.0 / math.sqrt(2.0 * math.pi))
        slope[r, :] = cdf + p * pdf
        transposed(p * cdf, r, act_th, act_tl)
    run(take_dy, 0, 4)
    round_2(1, dy_in)
    run(take_dy, 4, 7)
    round_3(1, dy_in)
    run(take_dy, 7, 10)
    round_4(1, dy_in)
    run(take_dy, 10, 11)
    round_5(1)
    run(take_dy, 11, 16)

    def pack(raw, offset, rxh):
        def one(i, carry):
            rc = lax.div(i, NY)
            ry = lax.rem(i, NY)
            owner_y = lax.rem(y + ry, NY)
            owner_x = xh + rxh - 2 * xh * rxh
            owner_c = core + rc - 2 * core * rc
            owner = (owner_x * NY + owner_y) * 2 + owner_c
            for e in range(4):
                raw[((rc * 2 + rxh) * NY + ry) * 4 + e] = table[tab[offset + owner * 4 + e]]
            return carry

        lax.fori_loop(0, 2 * NY, one, 0)

    def mine(raw, rxh, ry, first, count):
        return raw.at[pl.ds((rxh * NY + ry) * 4 + first, count)]

    def swap_cores(w, raw, rxh):
        return send(raw.at[pl.ds((2 + rxh) * 16, 16)], core_buf.at[w, rxh], cp)

    def add_core(copy, w, raw, rxh):
        copy.wait_recv()
        raw[pl.ds(rxh * 16, 16)] = raw[pl.ds(rxh * 16, 16)] + core_buf[w, rxh]

    def y_far(w, raw, rxh):
        return (
            send(mine(raw, rxh, 2, 0, 2), y_buf.at[w, rxh, 0, pl.ds(0, 2)], yp),
            send(mine(raw, rxh, 2, 2, 2), y_buf.at[w, rxh, 1, pl.ds(0, 2)], ym),
        )

    def y_near(pair, w, raw, rxh):
        at = (rxh * NY + 1) * 4
        pair[0].wait_recv()
        raw[pl.ds(at, 2)] = raw[pl.ds(at, 2)] + y_buf[w, rxh, 0, pl.ds(0, 2)]
        one = send(mine(raw, rxh, 1, 0, 4), y_buf.at[w, rxh, 0, pl.ds(2, 4)], yp)
        at = (rxh * NY + 3) * 4 + 2
        pair[1].wait_recv()
        raw[pl.ds(at, 2)] = raw[pl.ds(at, 2)] + y_buf[w, rxh, 1, pl.ds(0, 2)]
        two = send(mine(raw, rxh, 3, 0, 4), y_buf.at[w, rxh, 1, pl.ds(2, 4)], ym)
        return one, two

    def y_home(pair, w, raw, rxh):
        at = rxh * NY * 4
        pair[0].wait_recv()
        pair[1].wait_recv()
        raw[pl.ds(at, 4)] = (
            raw[pl.ds(at, 4)] + y_buf[w, rxh, 0, pl.ds(2, 4)] + y_buf[w, rxh, 1, pl.ds(2, 4)]
        )

    def far(w, raw):
        return send(mine(raw, 1, 0, 0, 4), far_buf.at[w], hp)

    def rs_send(col, dz, half, link):
        peer = {"+": zp, "-": zm, "x": xp}[link]
        to = {"+": (col, dz - 1), "-": (col, dz + 1), "x": (1 - col, dz)}[link]
        r = rows[half] if half else pl.ds(0, 256)
        index = len(rs_slots)
        copy = send(gx.at[SLOT[(col, dz)], r], rs_buf.at[index, r], peer)
        rs_slots.append((copy, index, SLOT[to], r))
        return index

    rs_slots = []

    def rs_add(index):
        copy, at, slot, r = rs_slots[index]
        copy.wait_recv()
        gx[slot, r] = gx[slot, r] + rs_buf[at, r]

    pack(raw2, 256 + 64, 1)
    core_21 = swap_cores(1, raw2, 1)
    pack(raw2, 256 + 64, 0)
    core_20 = swap_cores(1, raw2, 0)

    for part in range(2):
        r = pl.ds(part * 128, 128)
        grad_pre = ga[r, :] * slope[r, :]
        high, low = split(grad_pre)
        gph[r, :] = high
        gpl[r, :] = low
        transposed(grad_pre, r, gp_th, gp_tl)

    run(grad_x, 15, 16)
    p4a = rs_send(1, 4, "a", "+")
    p4b = rs_send(1, -4, "b", "-")
    run(grad_x, 10, 15)
    o4a = rs_send(0, 4, "a", "+")
    o4b = rs_send(0, -4, "b", "-")

    add_core(core_21, 1, raw2, 1)
    far_21 = y_far(1, raw2, 1)
    add_core(core_20, 1, raw2, 0)
    far_20 = y_far(1, raw2, 0)

    run(grad_x, 0, 10)
    p0 = rs_send(1, 0, None, "x")
    rs_add(p4a)
    p3a = rs_send(1, 3, None, "+")
    rs_add(p4b)
    p3b = rs_send(1, -3, None, "-")
    rs_add(o4a)
    o3a = rs_send(0, 3, None, "+")
    rs_add(o4b)
    o3b = rs_send(0, -3, None, "-")

    run(take_w1, 0, 8)
    near_21 = y_near(far_21, 1, raw2, 1)
    near_20 = y_near(far_20, 1, raw2, 0)
    run(take_w1, 8, 16)
    pack(raw1, 256, 1)
    core_11 = swap_cores(0, raw1, 1)
    pack(raw1, 256, 0)
    core_10 = swap_cores(0, raw1, 0)

    rs_add(p3a)
    p2a = rs_send(1, 2, None, "+")
    rs_add(p3b)
    p2b = rs_send(1, -2, None, "-")
    add_core(core_11, 0, raw1, 1)
    far_11 = y_far(0, raw1, 1)
    add_core(core_10, 0, raw1, 0)
    far_10 = y_far(0, raw1, 0)
    rs_add(p0)
    rs_add(o3a)
    o2a = rs_send(0, 2, None, "+")
    rs_add(o3b)
    o2b = rs_send(0, -2, None, "-")
    y_home(near_21, 1, raw2, 1)
    far_2 = far(1, raw2)
    rs_add(p2a)
    p1a = rs_send(1, 1, None, "x")
    rs_add(p2b)
    p1b = rs_send(1, -1, None, "x")
    near_11 = y_near(far_11, 0, raw1, 1)
    y_home(near_20, 1, raw2, 0)
    near_10 = y_near(far_10, 0, raw1, 0)
    rs_add(o2a)
    rs_add(p1a)
    o1a = rs_send(0, 1, None, "+")
    rs_add(o2b)
    rs_add(p1b)
    o1b = rs_send(0, -1, None, "-")
    y_home(near_11, 0, raw1, 1)
    far_1 = far(0, raw1)
    far_2.wait_recv()
    g2_out[...] = raw2[pl.ds(0, 4)] + far_buf[1]
    rs_add(o1a)
    rs_add(o1b)
    gx_out[...] = gx[0]
    y_home(near_10, 0, raw1, 0)
    far_1.wait_recv()
    g1_out[...] = raw1[pl.ds(0, 4)] + far_buf[0]
    for copy in copies:
        copy.wait_send()
    assert len(copies) == N_COPIES


def index_tables(slots_one, slots_two):
    c = lax.axis_index("ch")
    z, xl = c // 2, c % 2
    held = jnp.array([dz % NZ for _, dz in SLOTS], jnp.int32)
    other = jnp.array([col for col, _ in SLOTS], jnp.int32)
    shard = ((z + held) % NZ) * 2 + jnp.where(other == 1, 1 - xl, xl)
    place = jnp.arange(128, dtype=jnp.int32)
    q, h = (place // 4) % 2, place % 4
    f = jnp.repeat(shard, 8) * 2 + q
    fills, lies = [], []
    for ids, names in ((slots_one, f * 4 + h), (slots_two, h * 32 + f)):
        same = ids.reshape(1, 64) == names.reshape(128, 1)
        entry = jnp.arange(64, dtype=jnp.int32).reshape(1, 64)
        fills.append(64 + jnp.sum(jnp.where(same, entry - 64, 0), axis=1))
        lies.append(128 + jnp.sum(jnp.where(same, place.reshape(128, 1) - 128, 0), axis=0))
    return jnp.concatenate(fills + lies).astype(jnp.int32)


def body(inputs, grad_out, blocks_one, slots_one, blocks_two, slots_two):
    tab = index_tables(slots_one, slots_two)
    w1 = blocks_one.reshape(64, 128, 128)
    w2 = blocks_two.reshape(64, 128, 128)
    vmem = pl.BlockSpec(memory_space=pltpu.VMEM)
    hbm = pl.BlockSpec(memory_space=pl.ANY)
    shapes = lambda *dims, kind=F32: pltpu.VMEM(dims, kind)
    half = functools.partial(shapes, kind=BF16)
    gx, g1, g2 = pl.pallas_call(
        kernel,
        name="ffn_backward",
        out_shape=(
            jax.ShapeDtypeStruct((256, 256), F32),
            jax.ShapeDtypeStruct((4, 128, 128), F32),
            jax.ShapeDtypeStruct((4, 128, 128), F32),
        ),
        in_specs=[pl.BlockSpec(memory_space=pltpu.SMEM), vmem, vmem, hbm, hbm],
        out_specs=(vmem, vmem, vmem),
        scratch_shapes=[
            shapes(65, 128, 128), shapes(65, 128, 128),
            shapes(16, 256, 256), shapes(16, 256, 256),
            half(16, 256, 512), half(16, 256, 512),
            half(512, 256), half(512, 256),
            shapes(129, 128, 128),
            half(256, 256), half(256, 256),
            shapes(256, 512), shapes(256, 512), shapes(256, 512),
            half(512, 256), half(512, 256), half(512, 256), half(512, 256),
            half(256, 512), half(256, 512),
            shapes(16, 256, 256), shapes(17, 256, 256),
            shapes(2, 2, 16, 128, 128), shapes(2, 2, 2, 6, 128, 128), shapes(2, 4, 128, 128),
            pltpu.SemaphoreType.DMA((N_COPIES,)),
            pltpu.SemaphoreType.DMA((N_COPIES,)),
            pltpu.SemaphoreType.DMA((2,)),
        ],
        compiler_params=pltpu.CompilerParams(
            collective_id=0, has_side_effects=True, vmem_limit_bytes=66_000_000
        ),
    )(tab, inputs, grad_out, w1, w2)
    factor = 1.0 / math.sqrt(inputs.shape[0] * lax.axis_size("tok"))
    grad_one = (jnp.swapaxes(g1, 1, 2) * factor).reshape(1, 1, 4, 128, 128)
    grad_two = (g2 * factor).reshape(1, 1, 4, 128, 128)
    return gx, grad_one, grad_two


def solution(mesh):
    in_specs = (
        P("tok", "ch"),
        P("tok", "ch"),
        P(None, "ch", None, None, None),
        P(None, "ch", None),
        P(None, "ch", None, None, None),
        P(None, "ch", None),
    )
    out_specs = (P("tok", "ch"), P("tok", "ch", None, None, None), P("tok", "ch", None, None, None))
    return jax.shard_map(body, mesh=mesh, in_specs=in_specs, out_specs=out_specs, check_vma=False)
```

```python
import functools
import math

import jax
import jax.numpy as jnp
from jax import lax
from jax.experimental import pallas as pl
from jax.experimental.pallas import tpu as pltpu
from jax.sharding import PartitionSpec as P

F32 = jnp.float32
BF16 = jnp.bfloat16
MESH = pl.DeviceIdType.MESH
NZ, NXL, NXH, NY = 8, 2, 2, 4

SLOTS = [
    (0, 0),
    (0, -1), (0, 1), (1, 0),
    (0, -2), (0, 2), (1, 1),
    (0, -3), (0, 3), (1, -1),
    (0, 4), (1, -2), (1, 2),
    (1, -3), (1, 3), (1, 4),
]
SLOT = {key: at for at, key in enumerate(SLOTS)}
SLOT[(0, -4)] = SLOT[(0, 4)]
SLOT[(1, -4)] = SLOT[(1, 4)]
NT = (((1,), (1,)), ((), ()))
NN = (((1,), (0,)), ((), ()))

N_COPIES = 60 + 30 + 22


def dot(a, b, dims):
    return lax.dot_general(a, b, dims, preferred_element_type=F32)


def split(v):
    high = v.astype(BF16)
    return high, (v - high.astype(F32)).astype(BF16)


def kernel(
    ids1, ids2, x_in, dy_in, w1_hbm, w2_hbm,
    gx_out, g1_out, g2_out,
    raw1, raw2, xg, dyg, w1h, w1l, w2h, w2l, table,
    sh, sl, pre, ga, slope, act_th, act_tl, gp_th, gp_tl, gph, gpl,
    gx, rs_buf, core_buf, y_buf, far_buf, fill_v, fill, slot_of,
    send_sem, recv_sem, local_sem,
):
    t = lax.axis_index("tok")
    c = lax.axis_index("ch")
    core = lax.rem(t, 2)
    y = lax.rem(lax.div(t, 2), NY)
    xh = lax.div(t, 2 * NY)
    xl = lax.rem(c, 2)
    z = lax.div(c, 2)

    def at_z(step):
        return (t, lax.rem(z + step, NZ) * 2 + xl)

    def at_y(step):
        return ((xh * NY + lax.rem(y + step, NY)) * 2 + core, c)

    zp, zm = at_z(1), at_z(NZ - 1)
    yp, ym = at_y(1), at_y(NY - 1)
    xp = (t, z * 2 + (1 - xl))
    cp = ((xh * NY + y) * 2 + (1 - core), c)
    hp = (((1 - xh) * NY + y) * 2 + core, c)

    fetches = [
        pltpu.make_async_copy(src, dst, local_sem.at[at])
        for at, (src, dst) in enumerate(
            (
                (x_in, xg.at[0]),
                (w1_hbm, raw1.at[pl.ds(0, 64)]),
                (dy_in, dyg.at[0]),
                (w2_hbm, raw2.at[pl.ds(0, 64)]),
            )
        )
    ]

    barrier = pltpu.get_barrier_semaphore()
    for peer in (zp, zm, xp, yp, ym, cp, hp):
        pl.semaphore_signal(barrier, inc=1, device_id=peer, device_id_type=MESH)
    for fetch in fetches:
        fetch.start()
    pl.semaphore_wait(barrier, 7)

    copies = []

    def send(src, dst, peer):
        at = len(copies)
        copy = pltpu.make_async_remote_copy(
            src_ref=src, dst_ref=dst, send_sem=send_sem.at[at], recv_sem=recv_sem.at[at],
            device_id=peer, device_id_type=MESH,
        )
        copy.start()
        copies.append(copy)
        return copy

    rows = {"a": pl.ds(0, 128), "b": pl.ds(128, 128)}
    arrivals = {}

    def forward(phase, source, col, dz, half, link):
        peer = {"+": zp, "-": zm, "x": xp}[link]
        to = {"+": (col, dz - 1), "-": (col, dz + 1), "x": (1 - col, dz)}[link]
        buf = xg if phase == 0 else dyg
        src = source if (col, dz) == (0, 0) else buf.at[SLOT[(col, dz)]]
        copy = send(src.at[rows[half]], buf.at[SLOT[to], rows[half]], peer)
        arrivals[(phase, SLOT[to], half)] = copy

    def arrive(phase, key, halves="ab"):
        for half in halves:
            arrivals[(phase, SLOT[key], half)].wait_recv()

    def open_phase(phase, source):
        for one, two in ("ab", "ba"):
            forward(phase, source, 0, 0, one, "+")
            forward(phase, source, 0, 0, two, "-")
            forward(phase, source, 0, 0, one, "x")

    def gather(phase, source, take, then):
        def hand_on(col, dz, half, links):
            arrive(phase, (col, dz), half)
            for link in links:
                forward(phase, source, col, dz, half, link)

        for one, two in ("ab", "ba"):
            hand_on(0, -1, one, "+")
            hand_on(0, 1, two, "-x")
        forward(phase, source, 0, -1, "a", "x")
        forward(phase, source, 0, -1, "b", "x")
        run(take, 1, 3)
        arrive(phase, (1, 0))
        run(take, 3, 4)
        for one, two in ("ab", "ba"):
            hand_on(0, -2, one, "+")
            hand_on(0, 2, two, "-")
        run(take, 4, 6)
        arrive(phase, (1, 1))
        run(take, 6, 7)
        hand_on(0, -3, "a", "+x")
        hand_on(0, 3, "b", "-x")
        hand_on(0, -3, "b", "x")
        hand_on(0, 3, "a", "x")
        hand_on(1, -1, "a", "+")
        hand_on(1, -1, "b", "+")
        forward(phase, source, 1, 1, "b", "-")
        forward(phase, source, 1, 1, "a", "-")
        run(take, 7, 10)
        hand_on(1, -3, "a", "+")
        arrive(phase, (0, 4))
        run(take, 10, 11)
        hand_on(1, 3, "b", "-")
        then()
        arrive(phase, (1, -2))
        arrive(phase, (1, 2))
        run(take, 11, 13)
        arrive(phase, (1, -3), "b")
        run(take, 13, 14)
        arrive(phase, (1, 3), "a")
        arrive(phase, (1, 4))
        run(take, 14, 16)

    def take_x(s, carry):
        for q in range(2):
            for h in range(4):
                high, low = split(raw1[fill[0, s * 8 + q * 4 + h]])
                w1h[s, pl.ds(q * 128, 128), pl.ds(h * 128, 128)] = high
                w1l[s, pl.ds(q * 128, 128), pl.ds(h * 128, 128)] = low
        high, low = split(xg[s])
        sh[...] = high
        sl[...] = low
        pre[...] += (
            dot(sh[...], w1h[s], NN) + dot(sh[...], w1l[s], NN) + dot(sl[...], w1h[s], NN)
        )
        return carry

    def to_table(s, th, tl):
        full = dot(th[...], sh[...], NN) + dot(th[...], sl[...], NN) + dot(tl[...], sh[...], NN)
        for q in range(2):
            for h in range(4):
                table[s * 8 + q * 4 + h] = full[h * 128 : h * 128 + 128, q * 128 : q * 128 + 128]

    def take_dy(s, carry):
        for q in range(2):
            for h in range(4):
                high, low = split(raw2[fill[1, s * 8 + q * 4 + h]])
                w2h[pl.ds(h * 128, 128), pl.ds(q * 128, 128)] = high
                w2l[pl.ds(h * 128, 128), pl.ds(q * 128, 128)] = low
        high, low = split(dyg[s])
        sh[...] = high
        sl[...] = low
        ga[...] += (
            dot(sh[...], w2h[...], NT) + dot(sh[...], w2l[...], NT) + dot(sl[...], w2h[...], NT)
        )
        to_table(s, act_th, act_tl)
        return carry

    def take_w1(s, carry):
        high, low = split(xg[s])
        sh[...] = high
        sl[...] = low
        to_table(s, gp_th, gp_tl)
        return carry

    def grad_x(s, carry):
        gx[s] = dot(gph[...], w1h[s], NT) + dot(gph[...], w1l[s], NT) + dot(gpl[...], w1h[s], NT)
        return carry

    def run(body, first, last):
        lax.fori_loop(first, last, body, 0)

    def transposed(value, r, th, tl):
        high, low = split(value.T)
        th[:, r] = high
        tl[:, r] = low

    def fill_tables():
        lane = lax.broadcasted_iota(jnp.int32, (1, 128), 1)
        place = lax.div(lane, 8)
        shard = jnp.zeros_like(lane)
        for s, (col, dz) in enumerate(SLOTS):
            its = lax.rem(z + (dz + NZ), NZ) * 2 + xl + col - 2 * xl * col
            shard = jnp.where(place == s, its, shard)
            slot_of[col * NZ + (dz + NZ) % NZ] = jnp.int32(s)
        f = shard * 2 + lax.rem(lax.div(lane, 4), 2)
        h = lax.rem(lane, 4)
        one, two = f * 4 + h, h * 32 + f

        def owner(o, carry):
            a, b = carry
            for e in range(4):
                entry = o * 4 + e
                a = jnp.where(one == ids1[e, o], entry, a)
                b = jnp.where(two == ids2[e, o], entry, b)
            return a, b

        empty = jnp.full((1, 128), 64, jnp.int32)
        a, b = lax.fori_loop(0, 16, owner, (empty, empty))
        fill_v[0:1, :] = a
        fill_v[1:2, :] = b
        to_smem = pltpu.make_async_copy(fill_v, fill, local_sem.at[4])
        to_smem.start()
        to_smem.wait()

    open_phase(0, x_in)
    fill_tables()
    pre[...] = jnp.zeros_like(pre)
    ga[...] = jnp.zeros_like(ga)
    zero = jnp.zeros((128, 128), F32)
    raw1[64] = zero
    raw2[64] = zero
    table[128] = zero
    for fetch in fetches:
        fetch.wait()
    run(take_x, 0, 1)
    gather(0, x_in, take_x, lambda: open_phase(1, dy_in))
    for part in range(2):
        r = pl.ds(part * 128, 128)
        p = pre[r, :]
        cdf = 0.5 * (1.0 + lax.erf(p * (1.0 / math.sqrt(2.0))))
        pdf = jnp.exp(-0.5 * p * p) * (1.0 / math.sqrt(2.0 * math.pi))
        slope[r, :] = cdf + p * pdf
        transposed(p * cdf, r, act_th, act_tl)
    run(take_dy, 0, 1)
    gather(1, dy_in, take_dy, lambda: None)

    def lies(w, o, e):
        if w == 0:
            name = ids1[e, o]
            f, h = lax.div(name, 4), lax.rem(name, 4)
        else:
            name = ids2[e, o]
            f, h = lax.rem(name, 32), lax.div(name, 32)
        shard, q = lax.div(f, 2), lax.rem(f, 2)
        dz = lax.rem(lax.div(shard, 2) + (NZ - z), NZ)
        xs = lax.rem(shard, 2)
        slot = slot_of[(xs + xl - 2 * xs * xl) * NZ + dz]
        return jnp.where(name < 128, slot * 8 + q * 4 + h, 128)

    def pack(w, raw, rxh):
        def one(i, carry):
            rc = lax.div(i, NY)
            ry = lax.rem(i, NY)
            owner_y = lax.rem(y + ry, NY)
            owner_x = xh + rxh - 2 * xh * rxh
            owner_c = core + rc - 2 * core * rc
            owner = (owner_x * NY + owner_y) * 2 + owner_c
            for e in range(4):
                raw[((rc * 2 + rxh) * NY + ry) * 4 + e] = table[lies(w, owner, e)]
            return carry

        lax.fori_loop(0, 2 * NY, one, 0)

    def mine(raw, rxh, ry, first, count):
        return raw.at[pl.ds((rxh * NY + ry) * 4 + first, count)]

    def swap_cores(w, raw, rxh):
        return send(raw.at[pl.ds((2 + rxh) * 16, 16)], core_buf.at[w, rxh], cp)

    def add_core(copy, w, raw, rxh):
        copy.wait_recv()
        raw[pl.ds(rxh * 16, 16)] = raw[pl.ds(rxh * 16, 16)] + core_buf[w, rxh]

    def y_far(w, raw, rxh):
        return (
            send(mine(raw, rxh, 2, 0, 2), y_buf.at[w, rxh, 0, pl.ds(0, 2)], yp),
            send(mine(raw, rxh, 2, 2, 2), y_buf.at[w, rxh, 1, pl.ds(0, 2)], ym),
        )

    def y_near(pair, w, raw, rxh):
        at = (rxh * NY + 1) * 4
        pair[0].wait_recv()
        raw[pl.ds(at, 2)] = raw[pl.ds(at, 2)] + y_buf[w, rxh, 0, pl.ds(0, 2)]
        one = send(mine(raw, rxh, 1, 0, 4), y_buf.at[w, rxh, 0, pl.ds(2, 4)], yp)
        at = (rxh * NY + 3) * 4 + 2
        pair[1].wait_recv()
        raw[pl.ds(at, 2)] = raw[pl.ds(at, 2)] + y_buf[w, rxh, 1, pl.ds(0, 2)]
        two = send(mine(raw, rxh, 3, 0, 4), y_buf.at[w, rxh, 1, pl.ds(2, 4)], ym)
        return one, two

    def y_home(pair, w, raw, rxh):
        at = rxh * NY * 4
        pair[0].wait_recv()
        pair[1].wait_recv()
        raw[pl.ds(at, 4)] = (
            raw[pl.ds(at, 4)] + y_buf[w, rxh, 0, pl.ds(2, 4)] + y_buf[w, rxh, 1, pl.ds(2, 4)]
        )

    def far(w, raw):
        return send(mine(raw, 1, 0, 0, 4), far_buf.at[w], hp)

    inbound = {}

    def rs_send(col, dz, half, link):
        peer = {"+": zp, "-": zm, "x": xp}[link]
        to = {"+": (col, dz - 1), "-": (col, dz + 1), "x": (1 - col, dz)}[link]
        at = len(inbound)
        copy = send(gx.at[SLOT[(col, dz)], rows[half]], rs_buf.at[at], peer)
        inbound[(col, dz, half)] = (copy, at, SLOT[to])

    def rs_add(col, dz, half):
        copy, at, slot = inbound[(col, dz, half)]
        copy.wait_recv()
        gx[slot, rows[half]] = gx[slot, rows[half]] + rs_buf[at]

    pack(1, raw2, 1)
    core_21 = swap_cores(1, raw2, 1)
    pack(1, raw2, 0)
    core_20 = swap_cores(1, raw2, 0)

    for part in range(2):
        r = pl.ds(part * 128, 128)
        grad_pre = ga[r, :] * slope[r, :]
        high, low = split(grad_pre)
        gph[r, :] = high
        gpl[r, :] = low
        transposed(grad_pre, r, gp_th, gp_tl)

    run(grad_x, 15, 16)
    rs_send(1, 4, "a", "+")
    rs_send(1, -4, "b", "-")
    run(grad_x, 13, 15)
    rs_send(1, 3, "b", "+")
    rs_send(1, -3, "a", "-")
    run(take_w1, 0, 3)
    add_core(core_21, 1, raw2, 1)
    far_21 = y_far(1, raw2, 1)
    add_core(core_20, 1, raw2, 0)
    far_20 = y_far(1, raw2, 0)
    run(take_w1, 3, 7)
    rs_add(1, 4, "a")
    rs_send(1, 3, "a", "+")
    rs_add(1, -4, "b")
    rs_send(1, -3, "b", "-")
    run(grad_x, 11, 13)
    run(grad_x, 3, 4)
    rs_send(1, 0, "a", "x")
    rs_send(1, 0, "b", "x")
    run(take_w1, 7, 10)
    rs_add(1, 3, "b")
    rs_send(1, 2, "b", "+")
    rs_add(1, -3, "a")
    rs_send(1, -2, "a", "-")
    near_21 = y_near(far_21, 1, raw2, 1)
    run(take_w1, 10, 16)
    pack(0, raw1, 1)
    core_11 = swap_cores(0, raw1, 1)
    pack(0, raw1, 0)
    core_10 = swap_cores(0, raw1, 0)
    rs_add(1, 3, "a")
    rs_send(1, 2, "a", "+")
    rs_add(1, -3, "b")
    rs_send(1, -2, "b", "-")
    run(grad_x, 6, 11)
    rs_send(0, 4, "a", "+")
    rs_send(0, -4, "b", "-")
    rs_send(0, 3, "b", "+")
    rs_send(0, -3, "a", "-")
    add_core(core_11, 0, raw1, 1)
    far_11 = y_far(0, raw1, 1)
    add_core(core_10, 0, raw1, 0)
    far_10 = y_far(0, raw1, 0)
    rs_add(1, 2, "b")
    rs_send(1, 1, "b", "x")
    rs_add(1, -2, "a")
    rs_send(1, -1, "a", "x")
    run(grad_x, 0, 3)
    run(grad_x, 4, 6)
    y_home(near_21, 1, raw2, 1)
    far_2 = far(1, raw2)
    rs_add(1, 2, "a")
    rs_send(1, 1, "a", "x")
    rs_add(1, -2, "b")
    rs_send(1, -1, "b", "x")
    near_11 = y_near(far_11, 0, raw1, 1)
    near_20 = y_near(far_20, 1, raw2, 0)
    rs_add(0, 4, "a")
    rs_send(0, 3, "a", "+")
    rs_add(0, -4, "b")
    rs_send(0, -3, "b", "-")
    near_10 = y_near(far_10, 0, raw1, 0)
    rs_add(1, 0, "a")
    rs_add(1, 0, "b")
    rs_add(0, 3, "b")
    rs_send(0, 2, "b", "+")
    rs_add(0, -3, "a")
    rs_send(0, -2, "a", "-")
    rs_add(0, 3, "a")
    rs_send(0, 2, "a", "+")
    rs_add(0, -3, "b")
    rs_send(0, -2, "b", "-")
    y_home(near_11, 0, raw1, 1)
    far_1 = far(0, raw1)
    rs_add(1, 1, "b")
    rs_add(0, 2, "b")
    rs_send(0, 1, "b", "+")
    rs_add(1, -1, "a")
    rs_add(0, -2, "a")
    rs_send(0, -1, "a", "-")
    rs_add(1, 1, "a")
    rs_add(0, 2, "a")
    rs_send(0, 1, "a", "+")
    rs_add(1, -1, "b")
    rs_add(0, -2, "b")
    rs_send(0, -1, "b", "-")
    y_home(near_20, 1, raw2, 0)
    far_2.wait_recv()
    g2_out[...] = raw2[pl.ds(0, 4)] + far_buf[1]
    rs_add(0, 1, "b")
    rs_add(0, -1, "a")
    rs_add(0, 1, "a")
    rs_add(0, -1, "b")
    gx_out[...] = gx[0]
    y_home(near_10, 0, raw1, 0)
    far_1.wait_recv()
    g1_out[...] = raw1[pl.ds(0, 4)] + far_buf[0]
    for copy in copies:
        copy.wait_send()
    assert len(copies) == N_COPIES


def finish(factor, gx_in, g1_in, g2_in, gx_out, g1_out, g2_out):
    gx_out[...] = gx_in[...]
    for e in range(4):
        g1_out[e] = g1_in[e].T * factor
        g2_out[e] = g2_in[e] * factor


def body(inputs, grad_out, blocks_one, slots_one, blocks_two, slots_two):
    w1 = blocks_one.reshape(64, 128, 128)
    w2 = blocks_two.reshape(64, 128, 128)
    vmem = pl.BlockSpec(memory_space=pltpu.VMEM)
    hbm = pl.BlockSpec(memory_space=pl.ANY)
    smem = pl.BlockSpec(memory_space=pltpu.SMEM)
    ids = lambda slots: slots.transpose(1, 2, 0).reshape(4, 16)
    results = (
        jax.ShapeDtypeStruct((256, 256), F32),
        jax.ShapeDtypeStruct((4, 128, 128), F32),
        jax.ShapeDtypeStruct((4, 128, 128), F32),
    )
    shapes = lambda *dims, kind=F32: pltpu.VMEM(dims, kind)
    half = functools.partial(shapes, kind=BF16)
    gx, g1, g2 = pl.pallas_call(
        kernel,
        name="ffn_backward",
        out_shape=results,
        in_specs=[smem, smem, hbm, hbm, hbm, hbm],
        out_specs=(vmem, vmem, vmem),
        scratch_shapes=[
            shapes(65, 128, 128), shapes(65, 128, 128),
            shapes(16, 256, 256), shapes(16, 256, 256),
            half(16, 256, 512), half(16, 256, 512),
            half(512, 256), half(512, 256),
            shapes(129, 128, 128),
            half(256, 256), half(256, 256),
            shapes(256, 512), shapes(256, 512), shapes(256, 512),
            half(512, 256), half(512, 256), half(512, 256), half(512, 256),
            half(256, 512), half(256, 512),
            shapes(16, 256, 256), shapes(30, 128, 256),
            shapes(2, 2, 16, 128, 128), shapes(2, 2, 2, 6, 128, 128), shapes(2, 4, 128, 128),
            shapes(2, 128, kind=jnp.int32), pltpu.SMEM((2, 128), jnp.int32), pltpu.SMEM((16,), jnp.int32),
            pltpu.SemaphoreType.DMA((N_COPIES,)),
            pltpu.SemaphoreType.DMA((N_COPIES,)),
            pltpu.SemaphoreType.DMA((5,)),
        ],
        compiler_params=pltpu.CompilerParams(
            collective_id=0, has_side_effects=True, vmem_limit_bytes=66_000_000
        ),
    )(ids(slots_one), ids(slots_two), inputs, grad_out, w1, w2)
    factor = 1.0 / math.sqrt(inputs.shape[0] * lax.axis_size("tok"))
    gx, g1, g2 = pl.pallas_call(
        functools.partial(finish, factor),
        name="ffn_finish",
        out_shape=results,
        in_specs=[vmem] * 3,
        out_specs=(vmem,) * 3,
    )(gx, g1, g2)
    return gx, g1.reshape(1, 1, 4, 128, 128), g2.reshape(1, 1, 4, 128, 128)


def solution(mesh):
    in_specs = (
        P("tok", "ch"),
        P("tok", "ch"),
        P(None, "ch", None, None, None),
        P(None, "ch", None),
        P(None, "ch", None, None, None),
        P(None, "ch", None),
    )
    out_specs = (P("tok", "ch"), P("tok", "ch", None, None, None), P("tok", "ch", None, None, None))
    return jax.shard_map(body, mesh=mesh, in_specs=in_specs, out_specs=out_specs, check_vma=False)
```

```python
import functools
import math

import jax
import jax.numpy as jnp
from jax import lax
from jax.experimental import pallas as pl
from jax.experimental.pallas import tpu as pltpu
from jax.sharding import PartitionSpec as P

F32 = jnp.float32
BF16 = jnp.bfloat16
MESH = pl.DeviceIdType.MESH
NZ, NXL, NXH, NY = 8, 2, 2, 4

SLOTS = [
    (0, 0),
    (0, -1), (0, 1), (1, 0),
    (0, -2), (0, 2), (1, 1),
    (0, -3), (0, 3), (1, -1),
    (0, 4), (1, -2), (1, 2),
    (1, -3), (1, 3), (1, 4),
]
SLOT = {key: at for at, key in enumerate(SLOTS)}
SLOT[(0, -4)] = SLOT[(0, 4)]
SLOT[(1, -4)] = SLOT[(1, 4)]
NT = (((1,), (1,)), ((), ()))
NN = (((1,), (0,)), ((), ()))

N_COPIES = 60 + 30 + 30


def dot(a, b, dims):
    return lax.dot_general(a, b, dims, preferred_element_type=F32)


def split(v):
    high = v.astype(BF16)
    return high, (v - high.astype(F32)).astype(BF16)


def kernel(
    ids1_in, ids2_in, x_in, dy_in, w1_hbm, w2_hbm,
    gx_out, g1_out, g2_out,
    raw1, raw2, xg, dyg, w1h, w1l, w2h, w2l, last_h, last_l, table,
    sh, sl, pre, ga, slope, act_th, act_tl, gp_th, gp_tl, gph, gpl,
    gx, rs_buf, core_buf, y_buf, far_buf, fill_v, fill, slot_of, ids1, ids2, where1, where2,
    send_sem, recv_sem, local_sem,
):
    t = lax.axis_index("tok")
    c = lax.axis_index("ch")
    core = lax.rem(t, 2)
    y = lax.rem(lax.div(t, 2), NY)
    xh = lax.div(t, 2 * NY)
    xl = lax.rem(c, 2)
    z = lax.div(c, 2)

    def at_z(step):
        return (t, lax.rem(z + step, NZ) * 2 + xl)

    def at_y(step):
        return ((xh * NY + lax.rem(y + step, NY)) * 2 + core, c)

    zp, zm = at_z(1), at_z(NZ - 1)
    yp, ym = at_y(1), at_y(NY - 1)
    xp = (t, z * 2 + (1 - xl))
    cp = ((xh * NY + y) * 2 + (1 - core), c)
    hp = (((1 - xh) * NY + y) * 2 + core, c)

    fetches = [
        pltpu.make_async_copy(src, dst, local_sem.at[at])
        for at, (src, dst) in enumerate(
            (
                (ids1_in, ids1),
                (ids2_in, ids2),
                (x_in, xg.at[0]),
                (w1_hbm, raw1.at[pl.ds(0, 64)]),
                (dy_in, dyg.at[0]),
                (w2_hbm, raw2.at[pl.ds(0, 64)]),
            )
        )
    ]

    barrier = pltpu.get_barrier_semaphore()
    for peer in (zp, zm, xp, yp, ym, cp, hp):
        pl.semaphore_signal(barrier, inc=1, device_id=peer, device_id_type=MESH)
    for fetch in fetches:
        fetch.start()
    pl.semaphore_wait(barrier, 7)

    copies = []
    sent = {
        0: xg.at[pl.ds(0, 15)], 1: dyg.at[pl.ds(0, 15)], 2: rs_buf,
        3: core_buf.at[0], 4: core_buf.at[1], 5: y_buf.at[0], 6: y_buf.at[1],
        7: far_buf.at[0], 8: far_buf.at[1],
    }

    def all_sent(group):
        whole = sent[group]
        pltpu.make_async_remote_copy(
            src_ref=whole, dst_ref=whole, send_sem=send_sem.at[group], recv_sem=recv_sem.at[0],
            device_id=zp, device_id_type=MESH,
        ).wait_send()


    def send(src, dst, peer, group):
        at = len(copies)
        copy = pltpu.make_async_remote_copy(
            src_ref=src, dst_ref=dst, send_sem=send_sem.at[group], recv_sem=recv_sem.at[at],
            device_id=peer, device_id_type=MESH,
        )
        copy.start()
        copies.append(copy)
        return copy

    rows = {"a": pl.ds(0, 128), "b": pl.ds(128, 128)}
    arrivals = {}

    def forward(phase, source, col, dz, half, link):
        peer = {"+": zp, "-": zm, "x": xp}[link]
        to = {"+": (col, dz - 1), "-": (col, dz + 1), "x": (1 - col, dz)}[link]
        buf = xg if phase == 0 else dyg
        src = source if (col, dz) == (0, 0) else buf.at[SLOT[(col, dz)]]
        copy = send(src.at[rows[half]], buf.at[SLOT[to], rows[half]], peer, phase)
        arrivals[(phase, SLOT[to], half)] = copy

    def arrive(phase, key, halves="ab"):
        for half in halves:
            arrivals[(phase, SLOT[key], half)].wait_recv()

    def open_phase(phase, source):
        for one, two in ("ab", "ba"):
            forward(phase, source, 0, 0, one, "+")
            forward(phase, source, 0, 0, two, "-")
            forward(phase, source, 0, 0, one, "x")

    def gather(phase, source, take, take_last, then):
        def hand_on(col, dz, half, links):
            arrive(phase, (col, dz), half)
            for link in links:
                forward(phase, source, col, dz, half, link)

        for one, two in ("ab", "ba"):
            hand_on(0, -1, one, "+")
            hand_on(0, 1, two, "-x")
        forward(phase, source, 0, -1, "a", "x")
        forward(phase, source, 0, -1, "b", "x")
        run(take, 1, 3)
        arrive(phase, (1, 0))
        run(take, 3, 4)
        for one, two in ("ab", "ba"):
            hand_on(0, -2, one, "+")
            hand_on(0, 2, two, "-")
        run(take, 4, 6)
        arrive(phase, (1, 1))
        run(take, 6, 7)
        hand_on(0, -3, "a", "+x")
        hand_on(0, 3, "b", "-x")
        hand_on(0, -3, "b", "x")
        hand_on(0, 3, "a", "x")
        hand_on(1, -1, "a", "+")
        hand_on(1, -1, "b", "+")
        forward(phase, source, 1, 1, "b", "-")
        forward(phase, source, 1, 1, "a", "-")
        run(take, 7, 10)
        hand_on(1, -3, "a", "+")
        arrive(phase, (0, 4))
        run(take, 10, 11)
        hand_on(1, 3, "b", "-")
        then()
        arrive(phase, (1, -2))
        arrive(phase, (1, 2))
        run(take, 11, 13)
        arrive(phase, (1, -3), "b")
        run(take, 13, 14)
        arrive(phase, (1, 3), "a")
        arrive(phase, (1, 4))
        run(take_last, 14, 16)

    def take_x(s, carry):
        for q in range(2):
            for h in range(4):
                high, low = split(raw1[fill[0, s * 8 + q * 4 + h]])
                w1h[s, pl.ds(q * 128, 128), pl.ds(h * 128, 128)] = high
                w1l[s, pl.ds(q * 128, 128), pl.ds(h * 128, 128)] = low
        high, low = split(xg[s])
        sh[...] = high
        sl[...] = low
        pre[...] += (
            dot(sh[...], w1h[s], NN) + dot(sh[...], w1l[s], NN) + dot(sl[...], w1h[s], NN)
        )
        return carry

    def to_table(s, th, tl):
        full = dot(th[...], sh[...], NN) + dot(th[...], sl[...], NN) + dot(tl[...], sh[...], NN)
        for q in range(2):
            for h in range(4):
                table[s * 8 + q * 4 + h] = full[h * 128 : h * 128 + 128, q * 128 : q * 128 + 128]

    def load_dy(s):
        high, low = split(dyg[s])
        sh[...] = high
        sl[...] = low

    def fill_w2(s, to_h, to_l):
        for q in range(2):
            for h in range(4):
                high, low = split(raw2[fill[1, s * 8 + q * 4 + h]])
                to_h[pl.ds(h * 128, 128), pl.ds(q * 128, 128)] = high
                to_l[pl.ds(h * 128, 128), pl.ds(q * 128, 128)] = low

    def add_ga(wh, wl):
        ga[...] += dot(sh[...], wh[...], NT) + dot(sh[...], wl[...], NT) + dot(sl[...], wh[...], NT)

    def take_dy(s, carry):
        load_dy(s)
        fill_w2(s, w2h, w2l)
        add_ga(w2h, w2l)
        to_table(s, act_th, act_tl)
        return carry

    def fill_last(i, carry):
        fill_w2(14 + i, last_h.at[i], last_l.at[i])
        return carry

    def take_ga(s, carry):
        load_dy(s)
        add_ga(last_h.at[s - 14], last_l.at[s - 14])
        return carry

    def take_dw2(s, carry):
        load_dy(s)
        to_table(s, act_th, act_tl)
        return carry

    def take_w1(s, carry):
        high, low = split(xg[s])
        sh[...] = high
        sl[...] = low
        to_table(s, gp_th, gp_tl)
        return carry

    def grad_x(s, carry):
        gx[s] = dot(gph[...], w1h[s], NT) + dot(gph[...], w1l[s], NT) + dot(gpl[...], w1h[s], NT)
        return carry

    def run(body, first, last):
        lax.fori_loop(first, last, body, 0)

    def transposed(value, r, th, tl):
        high, low = split(value.T)
        th[:, r] = high
        tl[:, r] = low

    def lies(w, o, e):
        if w == 0:
            name = ids1[e, o]
            f, h = lax.div(name, 4), lax.rem(name, 4)
        else:
            name = ids2[e, o]
            f, h = lax.rem(name, 32), lax.div(name, 32)
        shard, q = lax.div(f, 2), lax.rem(f, 2)
        dz = lax.rem(lax.div(shard, 2) + (NZ - z), NZ)
        xs = lax.rem(shard, 2)
        slot = slot_of[(xs + xl - 2 * xs * xl) * NZ + dz]
        return jnp.where(name < 128, slot * 8 + q * 4 + h, 128)

    def fill_tables():
        lane = lax.broadcasted_iota(jnp.int32, (1, 128), 1)
        place = lax.div(lane, 8)
        shard = jnp.zeros_like(lane)
        for s, (col, dz) in enumerate(SLOTS):
            its = lax.rem(z + (dz + NZ), NZ) * 2 + xl + col - 2 * xl * col
            shard = jnp.where(place == s, its, shard)
            slot_of[col * NZ + (dz + NZ) % NZ] = jnp.int32(s)
        f = shard * 2 + lax.rem(lax.div(lane, 4), 2)
        h = lax.rem(lane, 4)
        one, two = f * 4 + h, h * 32 + f

        def owner(o, carry):
            a, b = carry
            for e in range(4):
                entry = o * 4 + e
                a = jnp.where(one == ids1[e, o], entry, a)
                b = jnp.where(two == ids2[e, o], entry, b)
            return a, b

        empty = jnp.full((1, 128), 64, jnp.int32)
        a, b = lax.fori_loop(0, 16, owner, (empty, empty))
        fill_v[0:1, :] = a
        fill_v[1:2, :] = b
        to_smem = pltpu.make_async_copy(fill_v, fill, local_sem.at[6])
        to_smem.start()
        to_smem.wait()

    def find_entries():
        def owner(o, carry):
            for e in range(4):
                where1[o * 4 + e] = lies(0, o, e)
                where2[o * 4 + e] = lies(1, o, e)
            return carry

        lax.fori_loop(0, 16, owner, 0)

    open_phase(0, x_in)
    fetches[0].wait()
    fetches[1].wait()
    fill_tables()
    pre[...] = jnp.zeros_like(pre)
    ga[...] = jnp.zeros_like(ga)
    zero = jnp.zeros((128, 128), F32)
    raw1[64] = zero
    raw2[64] = zero
    table[128] = zero
    for fetch in fetches[2:]:
        fetch.wait()
    run(take_x, 0, 1)

    def next_phase():
        open_phase(1, dy_in)
        find_entries()

    gather(0, x_in, take_x, take_x, next_phase)
    for part in range(2):
        r = pl.ds(part * 128, 128)
        p = pre[r, :]
        cdf = 0.5 * (1.0 + lax.erf(p * (1.0 / math.sqrt(2.0))))
        pdf = jnp.exp(-0.5 * p * p) * (1.0 / math.sqrt(2.0 * math.pi))
        slope[r, :] = cdf + p * pdf
        transposed(p * cdf, r, act_th, act_tl)
    run(take_dy, 0, 1)
    gather(1, dy_in, take_dy, take_dw2, lambda: run(fill_last, 0, 2))

    def pack(w, raw, rxh, first, last):
        where = where2 if w else where1

        def one(i, carry):
            rc = lax.rem(i, 2)
            ry = lax.div(i, 2)
            owner_y = lax.rem(y + ry, NY)
            owner_x = xh + rxh - 2 * xh * rxh
            owner_c = core + rc - 2 * core * rc
            owner = (owner_x * NY + owner_y) * 2 + owner_c
            for e in range(4):
                raw[((rc * 2 + rxh) * NY + ry) * 4 + e] = table[where[owner * 4 + e]]
            return carry

        lax.fori_loop(2 * first, 2 * last, one, 0)

    def mine(raw, rxh, ry, first, count):
        return raw.at[pl.ds((rxh * NY + ry) * 4 + first, count)]

    def swap_cores(w, raw, rxh, first, last):
        r = pl.ds(first * 4, (last - first) * 4)
        theirs = pl.ds(((2 + rxh) * NY + first) * 4, (last - first) * 4)
        return send(raw.at[theirs], core_buf.at[w, rxh, r], cp, 3 + w), first, last

    def add_core(swap, w, raw, rxh):
        copy, first, last = swap
        copy.wait_recv()
        ours = pl.ds((rxh * NY + first) * 4, (last - first) * 4)
        raw[ours] = raw[ours] + core_buf[w, rxh, pl.ds(first * 4, (last - first) * 4)]

    def swap_all(w, raw):
        swaps = {}
        for rxh, first, last in ((1, 2, 3), (0, 2, 3), (1, 3, 4), (1, 0, 2), (0, 3, 4), (0, 0, 2)):
            pack(w, raw, rxh, first, last)
            swaps[(rxh, first)] = swap_cores(w, raw, rxh, first, last)
        return swaps

    def y_far(w, raw, rxh):
        return (
            send(mine(raw, rxh, 2, 0, 2), y_buf.at[w, rxh, 0, pl.ds(0, 2)], yp, 5 + w),
            send(mine(raw, rxh, 2, 2, 2), y_buf.at[w, rxh, 1, pl.ds(0, 2)], ym, 5 + w),
        )

    def y_near(pair, w, raw, rxh):
        at = (rxh * NY + 1) * 4
        pair[0].wait_recv()
        raw[pl.ds(at, 2)] = raw[pl.ds(at, 2)] + y_buf[w, rxh, 0, pl.ds(0, 2)]
        one = send(mine(raw, rxh, 1, 0, 4), y_buf.at[w, rxh, 0, pl.ds(2, 4)], yp, 5 + w)
        at = (rxh * NY + 3) * 4 + 2
        pair[1].wait_recv()
        raw[pl.ds(at, 2)] = raw[pl.ds(at, 2)] + y_buf[w, rxh, 1, pl.ds(0, 2)]
        two = send(mine(raw, rxh, 3, 0, 4), y_buf.at[w, rxh, 1, pl.ds(2, 4)], ym, 5 + w)
        return one, two

    def y_home(pair, w, raw, rxh):
        at = rxh * NY * 4
        pair[0].wait_recv()
        pair[1].wait_recv()
        raw[pl.ds(at, 4)] = (
            raw[pl.ds(at, 4)] + y_buf[w, rxh, 0, pl.ds(2, 4)] + y_buf[w, rxh, 1, pl.ds(2, 4)]
        )

    def far(w, raw):
        return send(mine(raw, 1, 0, 0, 4), far_buf.at[w], hp, 7 + w)

    inbound = {}

    def rs_send(col, dz, half, link):
        peer = {"+": zp, "-": zm, "x": xp}[link]
        to = {"+": (col, dz - 1), "-": (col, dz + 1), "x": (1 - col, dz)}[link]
        at = len(inbound)
        copy = send(gx.at[SLOT[(col, dz)], rows[half]], rs_buf.at[at], peer, 2)
        inbound[(col, dz, half)] = (copy, at, SLOT[to])

    def rs_add(col, dz, half):
        copy, at, slot = inbound[(col, dz, half)]
        copy.wait_recv()
        gx[slot, rows[half]] = gx[slot, rows[half]] + rs_buf[at]

    swap_2 = swap_all(1, raw2)
    run(take_ga, 14, 16)
    for part in range(2):
        r = pl.ds(part * 128, 128)
        grad_pre = ga[r, :] * slope[r, :]
        high, low = split(grad_pre)
        gph[r, :] = high
        gpl[r, :] = low
        transposed(grad_pre, r, gp_th, gp_tl)
    run(grad_x, 15, 16)
    rs_send(1, 4, "a", "x")
    rs_send(1, 4, "b", "x")
    add_core(swap_2[(1, 2)], 1, raw2, 1)
    far_21 = y_far(1, raw2, 1)
    run(grad_x, 13, 15)
    rs_send(1, 3, "b", "+")
    rs_send(1, -3, "a", "-")
    rs_send(1, 3, "a", "+")
    rs_send(1, -3, "b", "-")
    add_core(swap_2[(0, 2)], 1, raw2, 0)
    far_20 = y_far(1, raw2, 0)
    run(take_w1, 0, 5)
    run(grad_x, 3, 4)
    rs_send(1, 0, "a", "x")
    rs_send(1, 0, "b", "x")
    add_core(swap_2[(1, 3)], 1, raw2, 1)
    add_core(swap_2[(1, 0)], 1, raw2, 1)
    add_core(swap_2[(0, 3)], 1, raw2, 0)
    add_core(swap_2[(0, 0)], 1, raw2, 0)
    run(grad_x, 11, 13)
    run(take_w1, 5, 6)
    near_21 = y_near(far_21, 1, raw2, 1)
    rs_add(1, 3, "b")
    rs_send(1, 2, "b", "+")
    rs_add(1, -3, "a")
    rs_send(1, -2, "a", "-")
    run(take_w1, 6, 11)
    rs_add(1, 3, "a")
    rs_send(1, 2, "a", "+")
    rs_add(1, -3, "b")
    rs_send(1, -2, "b", "-")
    run(take_w1, 11, 16)
    swap_1 = swap_all(0, raw1)
    run(grad_x, 10, 11)
    rs_add(1, 4, "a")
    rs_send(0, 4, "a", "+")
    rs_add(1, 4, "b")
    rs_send(0, -4, "b", "-")
    run(grad_x, 6, 10)
    rs_send(0, 3, "b", "+")
    rs_send(0, -3, "a", "-")
    rs_add(1, 2, "b")
    rs_send(1, 1, "b", "x")
    rs_add(1, -2, "a")
    rs_send(1, -1, "a", "x")
    add_core(swap_1[(1, 2)], 0, raw1, 1)
    far_11 = y_far(0, raw1, 1)
    add_core(swap_1[(0, 2)], 0, raw1, 0)
    far_10 = y_far(0, raw1, 0)
    rs_add(1, 2, "a")
    rs_send(1, 1, "a", "x")
    rs_add(1, -2, "b")
    rs_send(1, -1, "b", "x")
    y_home(near_21, 1, raw2, 1)
    far_2 = far(1, raw2)
    add_core(swap_1[(1, 3)], 0, raw1, 1)
    add_core(swap_1[(1, 0)], 0, raw1, 1)
    add_core(swap_1[(0, 3)], 0, raw1, 0)
    add_core(swap_1[(0, 0)], 0, raw1, 0)
    run(grad_x, 0, 3)
    run(grad_x, 4, 6)
    near_11 = y_near(far_11, 0, raw1, 1)
    near_20 = y_near(far_20, 1, raw2, 0)
    rs_add(0, 4, "a")
    rs_send(0, 3, "a", "+")
    rs_add(0, -4, "b")
    rs_send(0, -3, "b", "-")
    near_10 = y_near(far_10, 0, raw1, 0)
    rs_add(1, 0, "a")
    rs_add(1, 0, "b")
    all_sent(0)
    all_sent(1)
    rs_add(0, 3, "b")
    rs_send(0, 2, "b", "+")
    rs_add(0, -3, "a")
    rs_send(0, -2, "a", "-")
    rs_add(0, 3, "a")
    rs_send(0, 2, "a", "+")
    rs_add(0, -3, "b")
    rs_send(0, -2, "b", "-")
    y_home(near_11, 0, raw1, 1)
    far_1 = far(0, raw1)
    rs_add(1, 1, "b")
    rs_add(0, 2, "b")
    rs_send(0, 1, "b", "+")
    rs_add(1, -1, "a")
    rs_add(0, -2, "a")
    rs_send(0, -1, "a", "-")
    rs_add(1, 1, "a")
    rs_add(0, 2, "a")
    rs_send(0, 1, "a", "+")
    rs_add(1, -1, "b")
    rs_add(0, -2, "b")
    rs_send(0, -1, "b", "-")
    y_home(near_20, 1, raw2, 0)
    far_2.wait_recv()
    raw2[pl.ds(0, 4)] = raw2[pl.ds(0, 4)] + far_buf[1]
    put_g2 = pltpu.make_async_copy(raw2.at[pl.ds(0, 4)], g2_out, local_sem.at[7])
    put_g2.start()
    rs_add(0, 1, "b")
    rs_add(0, -1, "a")
    rs_add(0, 1, "a")
    rs_add(0, -1, "b")
    put_gx = pltpu.make_async_copy(gx.at[0], gx_out, local_sem.at[8])
    put_gx.start()
    y_home(near_10, 0, raw1, 0)
    far_1.wait_recv()
    raw1[pl.ds(0, 4)] = raw1[pl.ds(0, 4)] + far_buf[0]
    put_g1 = pltpu.make_async_copy(raw1.at[pl.ds(0, 4)], g1_out, local_sem.at[9])
    put_g1.start()
    for group in range(2, 9):
        all_sent(group)
    put_g2.wait()
    put_gx.wait()
    put_g1.wait()
    assert len(copies) == N_COPIES


def finish(factor, gx_in, g1_in, g2_in, gx_out, g1_out, g2_out):
    gx_out[...] = gx_in[...]
    for e in range(4):
        g1_out[e] = g1_in[e].T * factor
        g2_out[e] = g2_in[e] * factor


def body(inputs, grad_out, blocks_one, slots_one, blocks_two, slots_two):
    w1 = blocks_one.reshape(64, 128, 128)
    w2 = blocks_two.reshape(64, 128, 128)
    vmem = pl.BlockSpec(memory_space=pltpu.VMEM)
    hbm = pl.BlockSpec(memory_space=pltpu.HBM)
    ids = lambda slots: slots.transpose(1, 2, 0).reshape(4, 16)
    results = (
        jax.ShapeDtypeStruct((256, 256), F32),
        jax.ShapeDtypeStruct((4, 128, 128), F32),
        jax.ShapeDtypeStruct((4, 128, 128), F32),
    )
    shapes = lambda *dims, kind=F32: pltpu.VMEM(dims, kind)
    half = functools.partial(shapes, kind=BF16)
    gx, g1, g2 = pl.pallas_call(
        kernel,
        name="ffn_backward",
        out_shape=results,
        in_specs=[hbm] * 6,
        out_specs=(hbm,) * 3,
        scratch_shapes=[
            shapes(65, 128, 128), shapes(65, 128, 128),
            shapes(16, 256, 256), shapes(16, 256, 256),
            half(16, 256, 512), half(16, 256, 512),
            half(512, 256), half(512, 256), half(2, 512, 256), half(2, 512, 256),
            shapes(129, 128, 128),
            half(256, 256), half(256, 256),
            shapes(256, 512), shapes(256, 512), shapes(256, 512),
            half(512, 256), half(512, 256), half(512, 256), half(512, 256),
            half(256, 512), half(256, 512),
            shapes(16, 256, 256), shapes(30, 128, 256),
            shapes(2, 2, 16, 128, 128), shapes(2, 2, 2, 6, 128, 128), shapes(2, 4, 128, 128),
            shapes(2, 128, kind=jnp.int32), pltpu.SMEM((2, 128), jnp.int32), pltpu.SMEM((16,), jnp.int32),
            pltpu.SMEM((4, 16), jnp.int32), pltpu.SMEM((4, 16), jnp.int32),
            pltpu.SMEM((64,), jnp.int32), pltpu.SMEM((64,), jnp.int32),
            pltpu.SemaphoreType.DMA((9,)),
            pltpu.SemaphoreType.DMA((N_COPIES,)),
            pltpu.SemaphoreType.DMA((10,)),
        ],
        compiler_params=pltpu.CompilerParams(
            collective_id=0, has_side_effects=True, vmem_limit_bytes=60_000_000
        ),
    )(ids(slots_one), ids(slots_two), inputs, grad_out, w1, w2)
    factor = 1.0 / math.sqrt(inputs.shape[0] * lax.axis_size("tok"))
    gx, g1, g2 = pl.pallas_call(
        functools.partial(finish, factor),
        name="ffn_finish",
        out_shape=results,
        in_specs=[vmem] * 3,
        out_specs=(vmem,) * 3,
    )(gx, g1, g2)
    return gx, g1.reshape(1, 1, 4, 128, 128), g2.reshape(1, 1, 4, 128, 128)


def solution(mesh):
    in_specs = (
        P("tok", "ch"),
        P("tok", "ch"),
        P(None, "ch", None, None, None),
        P(None, "ch", None),
        P(None, "ch", None, None, None),
        P(None, "ch", None),
    )
    out_specs = (P("tok", "ch"), P("tok", "ch", None, None, None), P("tok", "ch", None, None, None))
    return jax.shard_map(body, mesh=mesh, in_specs=in_specs, out_specs=out_specs, check_vma=False)
```

```python
import functools
import math

import jax
import jax.numpy as jnp
from jax import lax
from jax.experimental import pallas as pl
from jax.experimental.pallas import tpu as pltpu
from jax.sharding import PartitionSpec as P

F32 = jnp.float32
BF16 = jnp.bfloat16
MESH = pl.DeviceIdType.MESH
NZ, NXL, NXH, NY = 8, 2, 2, 4

SLOTS = [
    (0, 0),
    (0, -1), (0, 1), (1, 0),
    (0, -2), (0, 2), (1, 1),
    (0, -3), (0, 3), (1, -1),
    (0, 4), (1, -2), (1, 2),
    (1, -3), (1, 3), (1, 4),
]
SLOT = {key: at for at, key in enumerate(SLOTS)}
SLOT[(0, -4)] = SLOT[(0, 4)]
SLOT[(1, -4)] = SLOT[(1, 4)]
NT = (((1,), (1,)), ((), ()))
NN = (((1,), (0,)), ((), ()))

N_COPIES = 60 + 30 + 30


def dot(a, b, dims):
    return lax.dot_general(a, b, dims, preferred_element_type=F32)


def split(v):
    high = v.astype(BF16)
    return high, (v - high.astype(F32)).astype(BF16)


def kernel(
    ids1_in, ids2_in, x_in, dy_in, w1_hbm, w2_hbm,
    gx_out, g1_out, g2_out,
    raw1, raw2, xg, dyg, w1h, w1l, w2h, w2l, last_h, last_l, table,
    sh, sl, pre, ga, slope, act_th, act_tl, gp_th, gp_tl, gph, gpl,
    gx, rs_buf, core_buf, y_buf, far_buf, fill_v, fill, slot_of, ids1, ids2, where1, where2,
    send_sem, recv_sem, local_sem,
):
    t = lax.axis_index("tok")
    c = lax.axis_index("ch")
    core = lax.rem(t, 2)
    y = lax.rem(lax.div(t, 2), NY)
    xh = lax.div(t, 2 * NY)
    xl = lax.rem(c, 2)
    z = lax.div(c, 2)

    def at_z(step):
        return (t, lax.rem(z + step, NZ) * 2 + xl)

    def at_y(step):
        return ((xh * NY + lax.rem(y + step, NY)) * 2 + core, c)

    zp, zm = at_z(1), at_z(NZ - 1)
    yp, ym = at_y(1), at_y(NY - 1)
    xp = (t, z * 2 + (1 - xl))
    cp = ((xh * NY + y) * 2 + (1 - core), c)
    hp = (((1 - xh) * NY + y) * 2 + core, c)

    fetches = [
        pltpu.make_async_copy(src, dst, local_sem.at[at])
        for at, (src, dst) in enumerate(
            (
                (ids1_in, ids1),
                (ids2_in, ids2),
                (x_in, xg.at[0]),
                (w1_hbm, raw1.at[pl.ds(0, 64)]),
                (dy_in, dyg.at[0]),
                (w2_hbm, raw2.at[pl.ds(0, 64)]),
            )
        )
    ]

    barrier = pltpu.get_barrier_semaphore()
    for peer in (zp, zm, xp, yp, ym, cp, hp):
        pl.semaphore_signal(barrier, inc=1, device_id=peer, device_id_type=MESH)
    for fetch in fetches:
        fetch.start()
    pl.semaphore_wait(barrier, 7)

    copies = []
    sent = {
        0: xg.at[pl.ds(0, 15)], 1: dyg.at[pl.ds(0, 15)], 2: rs_buf,
        3: core_buf.at[0], 4: core_buf.at[1], 5: y_buf.at[0], 6: y_buf.at[1],
        7: far_buf.at[0], 8: far_buf.at[1],
    }

    def all_sent(group):
        whole = sent[group]
        pltpu.make_async_remote_copy(
            src_ref=whole, dst_ref=whole, send_sem=send_sem.at[group], recv_sem=recv_sem.at[0],
            device_id=zp, device_id_type=MESH,
        ).wait_send()


    def send(src, dst, peer, group):
        at = len(copies)
        copy = pltpu.make_async_remote_copy(
            src_ref=src, dst_ref=dst, send_sem=send_sem.at[group], recv_sem=recv_sem.at[at],
            device_id=peer, device_id_type=MESH,
        )
        copy.start()
        copies.append(copy)
        return copy

    rows = {"a": pl.ds(0, 128), "b": pl.ds(128, 128)}
    arrivals = {}

    def forward(phase, source, col, dz, half, link):
        peer = {"+": zp, "-": zm, "x": xp}[link]
        to = {"+": (col, dz - 1), "-": (col, dz + 1), "x": (1 - col, dz)}[link]
        buf = xg if phase == 0 else dyg
        src = source if (col, dz) == (0, 0) else buf.at[SLOT[(col, dz)]]
        copy = send(src.at[rows[half]], buf.at[SLOT[to], rows[half]], peer, phase)
        arrivals[(phase, SLOT[to], half)] = copy

    def arrive(phase, key, halves="ab"):
        for half in halves:
            arrivals[(phase, SLOT[key], half)].wait_recv()

    def open_phase(phase, source):
        for one, two in ("ab", "ba"):
            forward(phase, source, 0, 0, one, "+")
            forward(phase, source, 0, 0, two, "-")
            forward(phase, source, 0, 0, one, "x")

    def gather(phase, source, take, take_last, then):
        def hand_on(col, dz, half, links):
            arrive(phase, (col, dz), half)
            for link in links:
                forward(phase, source, col, dz, half, link)

        for one, two in ("ab", "ba"):
            hand_on(0, -1, one, "+")
            hand_on(0, 1, two, "-x")
        forward(phase, source, 0, -1, "a", "x")
        forward(phase, source, 0, -1, "b", "x")
        run(take, 1, 3)
        arrive(phase, (1, 0))
        run(take, 3, 4)
        for one, two in ("ab", "ba"):
            hand_on(0, -2, one, "+")
            hand_on(0, 2, two, "-")
        run(take, 4, 6)
        arrive(phase, (1, 1))
        run(take, 6, 7)
        hand_on(0, -3, "a", "+x")
        hand_on(0, 3, "b", "-x")
        hand_on(0, -3, "b", "x")
        hand_on(0, 3, "a", "x")
        hand_on(1, -1, "a", "+")
        hand_on(1, -1, "b", "+")
        forward(phase, source, 1, 1, "b", "-")
        forward(phase, source, 1, 1, "a", "-")
        run(take, 7, 10)
        hand_on(1, -3, "a", "+")
        arrive(phase, (0, 4))
        run(take, 10, 11)
        hand_on(1, 3, "b", "-")
        then()
        arrive(phase, (1, -2))
        arrive(phase, (1, 2))
        run(take, 11, 13)
        arrive(phase, (1, -3), "b")
        run(take, 13, 14)
        arrive(phase, (1, 3), "a")
        arrive(phase, (1, 4))
        run(take_last, 14, 16)

    def take_x(s, carry):
        for q in range(2):
            for h in range(4):
                high, low = split(raw1[fill[0, s * 8 + q * 4 + h]])
                w1h[s, pl.ds(q * 128, 128), pl.ds(h * 128, 128)] = high
                w1l[s, pl.ds(q * 128, 128), pl.ds(h * 128, 128)] = low
        high, low = split(xg[s])
        sh[...] = high
        sl[...] = low
        pre[...] += (
            dot(sh[...], w1h[s], NN) + dot(sh[...], w1l[s], NN) + dot(sl[...], w1h[s], NN)
        )
        return carry

    def to_table(s, th, tl):
        full = dot(th[...], sh[...], NN) + dot(th[...], sl[...], NN) + dot(tl[...], sh[...], NN)
        for q in range(2):
            for h in range(4):
                table[s * 8 + q * 4 + h] = full[h * 128 : h * 128 + 128, q * 128 : q * 128 + 128]

    def load_dy(s):
        high, low = split(dyg[s])
        sh[...] = high
        sl[...] = low

    def fill_w2(s, to_h, to_l):
        for q in range(2):
            for h in range(4):
                high, low = split(raw2[fill[1, s * 8 + q * 4 + h]])
                to_h[pl.ds(h * 128, 128), pl.ds(q * 128, 128)] = high
                to_l[pl.ds(h * 128, 128), pl.ds(q * 128, 128)] = low

    def add_ga(wh, wl):
        ga[...] += dot(sh[...], wh[...], NT) + dot(sh[...], wl[...], NT) + dot(sl[...], wh[...], NT)

    def take_dy(s, carry):
        load_dy(s)
        fill_w2(s, w2h, w2l)
        add_ga(w2h, w2l)
        to_table(s, act_th, act_tl)
        return carry

    def fill_last(i, carry):
        fill_w2(14 + i, last_h.at[i], last_l.at[i])
        return carry

    def take_ga(s, carry):
        load_dy(s)
        add_ga(last_h.at[s - 14], last_l.at[s - 14])
        return carry

    def take_dw2(s, carry):
        load_dy(s)
        to_table(s, act_th, act_tl)
        return carry

    def take_w1(s, carry):
        high, low = split(xg[s])
        sh[...] = high
        sl[...] = low
        to_table(s, gp_th, gp_tl)
        return carry

    def grad_x(s, carry):
        gx[s] = dot(gph[...], w1h[s], NT) + dot(gph[...], w1l[s], NT) + dot(gpl[...], w1h[s], NT)
        return carry

    def run(body, first, last):
        lax.fori_loop(first, last, body, 0)

    def transposed(value, r, th, tl):
        high, low = split(value.T)
        th[:, r] = high
        tl[:, r] = low

    def lies(w, o, e):
        if w == 0:
            name = ids1[e, o]
            f, h = lax.div(name, 4), lax.rem(name, 4)
        else:
            name = ids2[e, o]
            f, h = lax.rem(name, 32), lax.div(name, 32)
        shard, q = lax.div(f, 2), lax.rem(f, 2)
        dz = lax.rem(lax.div(shard, 2) + (NZ - z), NZ)
        xs = lax.rem(shard, 2)
        slot = slot_of[(xs + xl - 2 * xs * xl) * NZ + dz]
        return jnp.where(name < 128, slot * 8 + q * 4 + h, 128)

    def fill_tables():
        lane = lax.broadcasted_iota(jnp.int32, (1, 128), 1)
        place = lax.div(lane, 8)
        shard = jnp.zeros_like(lane)
        for s, (col, dz) in enumerate(SLOTS):
            its = lax.rem(z + (dz + NZ), NZ) * 2 + xl + col - 2 * xl * col
            shard = jnp.where(place == s, its, shard)
            slot_of[col * NZ + (dz + NZ) % NZ] = jnp.int32(s)
        f = shard * 2 + lax.rem(lax.div(lane, 4), 2)
        h = lax.rem(lane, 4)
        one, two = f * 4 + h, h * 32 + f

        def owner(o, carry):
            a, b = carry
            for e in range(4):
                entry = o * 4 + e
                a = jnp.where(one == ids1[e, o], entry, a)
                b = jnp.where(two == ids2[e, o], entry, b)
            return a, b

        empty = jnp.full((1, 128), 64, jnp.int32)
        a, b = lax.fori_loop(0, 16, owner, (empty, empty))
        fill_v[0:1, :] = a
        fill_v[1:2, :] = b
        to_smem = pltpu.make_async_copy(fill_v, fill, local_sem.at[6])
        to_smem.start()
        to_smem.wait()

    def find_entries():
        def owner(o, carry):
            for e in range(4):
                where1[o * 4 + e] = lies(0, o, e)
                where2[o * 4 + e] = lies(1, o, e)
            return carry

        lax.fori_loop(0, 16, owner, 0)

    open_phase(0, x_in)
    fetches[0].wait()
    fetches[1].wait()
    fill_tables()
    pre[...] = jnp.zeros_like(pre)
    ga[...] = jnp.zeros_like(ga)
    zero = jnp.zeros((128, 128), F32)
    raw1[64] = zero
    raw2[64] = zero
    table[128] = zero
    for fetch in fetches[2:]:
        fetch.wait()
    run(take_x, 0, 1)

    def next_phase():
        open_phase(1, dy_in)
        find_entries()

    gather(0, x_in, take_x, take_x, next_phase)
    for part in range(2):
        r = pl.ds(part * 128, 128)
        p = pre[r, :]
        cdf = 0.5 * (1.0 + lax.erf(p * (1.0 / math.sqrt(2.0))))
        pdf = jnp.exp(-0.5 * p * p) * (1.0 / math.sqrt(2.0 * math.pi))
        slope[r, :] = cdf + p * pdf
        transposed(p * cdf, r, act_th, act_tl)
    run(take_dy, 0, 1)
    gather(1, dy_in, take_dy, take_dw2, lambda: run(fill_last, 0, 2))

    def pack(w, raw, rxh, first, last):
        where = where2 if w else where1

        def one(i, carry):
            rc = lax.rem(i, 2)
            ry = lax.div(i, 2)
            owner_y = lax.rem(y + ry, NY)
            owner_x = xh + rxh - 2 * xh * rxh
            owner_c = core + rc - 2 * core * rc
            owner = (owner_x * NY + owner_y) * 2 + owner_c
            for e in range(4):
                raw[((rc * 2 + rxh) * NY + ry) * 4 + e] = table[where[owner * 4 + e]]
            return carry

        lax.fori_loop(2 * first, 2 * last, one, 0)

    def mine(raw, rxh, ry, first, count):
        return raw.at[pl.ds((rxh * NY + ry) * 4 + first, count)]

    def swap_cores(w, raw, rxh, first, last):
        r = pl.ds(first * 4, (last - first) * 4)
        theirs = pl.ds(((2 + rxh) * NY + first) * 4, (last - first) * 4)
        return send(raw.at[theirs], core_buf.at[w, rxh, r], cp, 3 + w), first, last

    def add_core(swap, w, raw, rxh):
        copy, first, last = swap
        copy.wait_recv()
        ours = pl.ds((rxh * NY + first) * 4, (last - first) * 4)
        raw[ours] = raw[ours] + core_buf[w, rxh, pl.ds(first * 4, (last - first) * 4)]

    def swap_all(w, raw):
        swaps = {}
        for rxh, first, last in ((1, 2, 3), (0, 2, 3), (1, 3, 4), (1, 0, 2), (0, 3, 4), (0, 0, 2)):
            pack(w, raw, rxh, first, last)
            swaps[(rxh, first)] = swap_cores(w, raw, rxh, first, last)
        return swaps

    def y_far(w, raw, rxh):
        return (
            send(mine(raw, rxh, 2, 0, 2), y_buf.at[w, rxh, 0, pl.ds(0, 2)], yp, 5 + w),
            send(mine(raw, rxh, 2, 2, 2), y_buf.at[w, rxh, 1, pl.ds(0, 2)], ym, 5 + w),
        )

    def y_near(pair, w, raw, rxh):
        at = (rxh * NY + 1) * 4
        pair[0].wait_recv()
        raw[pl.ds(at, 2)] = raw[pl.ds(at, 2)] + y_buf[w, rxh, 0, pl.ds(0, 2)]
        one = send(mine(raw, rxh, 1, 0, 4), y_buf.at[w, rxh, 0, pl.ds(2, 4)], yp, 5 + w)
        at = (rxh * NY + 3) * 4 + 2
        pair[1].wait_recv()
        raw[pl.ds(at, 2)] = raw[pl.ds(at, 2)] + y_buf[w, rxh, 1, pl.ds(0, 2)]
        two = send(mine(raw, rxh, 3, 0, 4), y_buf.at[w, rxh, 1, pl.ds(2, 4)], ym, 5 + w)
        return one, two

    def y_home(pair, w, raw, rxh):
        at = rxh * NY * 4
        pair[0].wait_recv()
        pair[1].wait_recv()
        raw[pl.ds(at, 4)] = (
            raw[pl.ds(at, 4)] + y_buf[w, rxh, 0, pl.ds(2, 4)] + y_buf[w, rxh, 1, pl.ds(2, 4)]
        )

    def far(w, raw):
        return send(mine(raw, 1, 0, 0, 4), far_buf.at[w], hp, 7 + w)

    inbound = {}

    def rs_send(col, dz, half, link):
        peer = {"+": zp, "-": zm, "x": xp}[link]
        to = {"+": (col, dz - 1), "-": (col, dz + 1), "x": (1 - col, dz)}[link]
        at = len(inbound)
        copy = send(gx.at[SLOT[(col, dz)], rows[half]], rs_buf.at[at], peer, 2)
        inbound[(col, dz, half)] = (copy, at, SLOT[to])

    def rs_add(col, dz, half):
        copy, at, slot = inbound[(col, dz, half)]
        copy.wait_recv()
        gx[slot, rows[half]] = gx[slot, rows[half]] + rs_buf[at]

    swap_2 = swap_all(1, raw2)
    run(take_ga, 14, 16)
    for part in range(2):
        r = pl.ds(part * 128, 128)
        grad_pre = ga[r, :] * slope[r, :]
        high, low = split(grad_pre)
        gph[r, :] = high
        gpl[r, :] = low
        transposed(grad_pre, r, gp_th, gp_tl)
    run(grad_x, 15, 16)
    rs_send(1, 4, "a", "x")
    rs_send(1, 4, "b", "x")
    add_core(swap_2[(1, 2)], 1, raw2, 1)
    far_21 = y_far(1, raw2, 1)
    run(grad_x, 13, 15)
    rs_send(1, 3, "b", "+")
    rs_send(1, -3, "a", "-")
    rs_send(1, 3, "a", "+")
    rs_send(1, -3, "b", "-")
    run(take_w1, 0, 3)
    add_core(swap_2[(0, 2)], 1, raw2, 0)
    far_20 = y_far(1, raw2, 0)
    run(take_w1, 3, 5)
    run(grad_x, 3, 4)
    rs_send(1, 0, "a", "x")
    rs_send(1, 0, "b", "x")
    add_core(swap_2[(1, 3)], 1, raw2, 1)
    add_core(swap_2[(1, 0)], 1, raw2, 1)
    add_core(swap_2[(0, 3)], 1, raw2, 0)
    add_core(swap_2[(0, 0)], 1, raw2, 0)
    run(grad_x, 11, 13)
    run(take_w1, 5, 8)
    near_21 = y_near(far_21, 1, raw2, 1)
    rs_add(1, 3, "b")
    rs_send(1, 2, "b", "+")
    rs_add(1, -3, "a")
    rs_send(1, -2, "a", "-")
    run(take_w1, 8, 16)
    swap_1 = swap_all(0, raw1)
    rs_add(1, 3, "a")
    rs_send(1, 2, "a", "+")
    rs_add(1, -3, "b")
    rs_send(1, -2, "b", "-")
    run(grad_x, 10, 11)
    rs_add(1, 4, "a")
    rs_send(0, 4, "a", "+")
    rs_add(1, 4, "b")
    rs_send(0, -4, "b", "-")
    add_core(swap_1[(1, 2)], 0, raw1, 1)
    far_11 = y_far(0, raw1, 1)
    run(grad_x, 6, 10)
    rs_send(0, 3, "b", "+")
    rs_send(0, -3, "a", "-")
    rs_add(1, 2, "b")
    rs_send(1, 1, "b", "x")
    rs_add(1, -2, "a")
    rs_send(1, -1, "a", "x")
    add_core(swap_1[(0, 2)], 0, raw1, 0)
    far_10 = y_far(0, raw1, 0)
    y_home(near_21, 1, raw2, 1)
    rs_add(1, 2, "a")
    rs_send(1, 1, "a", "x")
    rs_add(1, -2, "b")
    rs_send(1, -1, "b", "x")
    far_2 = far(1, raw2)
    add_core(swap_1[(1, 3)], 0, raw1, 1)
    add_core(swap_1[(1, 0)], 0, raw1, 1)
    add_core(swap_1[(0, 3)], 0, raw1, 0)
    add_core(swap_1[(0, 0)], 0, raw1, 0)
    run(grad_x, 0, 3)
    run(grad_x, 4, 6)
    rs_add(0, 4, "a")
    rs_send(0, 3, "a", "+")
    rs_add(0, -4, "b")
    rs_send(0, -3, "b", "-")
    near_11 = y_near(far_11, 0, raw1, 1)
    near_20 = y_near(far_20, 1, raw2, 0)
    rs_add(1, 0, "a")
    rs_add(1, 0, "b")
    near_10 = y_near(far_10, 0, raw1, 0)
    all_sent(0)
    all_sent(1)
    rs_add(0, 3, "b")
    rs_send(0, 2, "b", "+")
    rs_add(0, -3, "a")
    rs_send(0, -2, "a", "-")
    rs_add(0, 3, "a")
    rs_send(0, 2, "a", "+")
    rs_add(0, -3, "b")
    rs_send(0, -2, "b", "-")
    y_home(near_11, 0, raw1, 1)
    far_1 = far(0, raw1)
    rs_add(1, 1, "b")
    rs_add(0, 2, "b")
    rs_send(0, 1, "b", "+")
    rs_add(1, -1, "a")
    rs_add(0, -2, "a")
    rs_send(0, -1, "a", "-")
    rs_add(1, 1, "a")
    rs_add(0, 2, "a")
    rs_send(0, 1, "a", "+")
    rs_add(1, -1, "b")
    rs_add(0, -2, "b")
    rs_send(0, -1, "b", "-")
    y_home(near_20, 1, raw2, 0)
    far_2.wait_recv()
    raw2[pl.ds(0, 4)] = raw2[pl.ds(0, 4)] + far_buf[1]
    put_g2 = pltpu.make_async_copy(raw2.at[pl.ds(0, 4)], g2_out, local_sem.at[7])
    put_g2.start()
    rs_add(0, 1, "b")
    rs_add(0, -1, "a")
    rs_add(0, 1, "a")
    rs_add(0, -1, "b")
    put_gx = pltpu.make_async_copy(gx.at[0], gx_out, local_sem.at[8])
    put_gx.start()
    y_home(near_10, 0, raw1, 0)
    far_1.wait_recv()
    raw1[pl.ds(0, 4)] = raw1[pl.ds(0, 4)] + far_buf[0]
    put_g1 = pltpu.make_async_copy(raw1.at[pl.ds(0, 4)], g1_out, local_sem.at[9])
    put_g1.start()
    for group in range(2, 9):
        all_sent(group)
    put_g2.wait()
    put_gx.wait()
    put_g1.wait()
    assert len(copies) == N_COPIES


def finish(factor, gx_in, g1_in, g2_in, gx_out, g1_out, g2_out):
    gx_out[...] = gx_in[...]
    for e in range(4):
        g1_out[e] = g1_in[e].T * factor
        g2_out[e] = g2_in[e] * factor


def body(inputs, grad_out, blocks_one, slots_one, blocks_two, slots_two):
    w1 = blocks_one.reshape(64, 128, 128)
    w2 = blocks_two.reshape(64, 128, 128)
    vmem = pl.BlockSpec(memory_space=pltpu.VMEM)
    hbm = pl.BlockSpec(memory_space=pltpu.HBM)
    ids = lambda slots: slots.transpose(1, 2, 0).reshape(4, 16)
    results = (
        jax.ShapeDtypeStruct((256, 256), F32),
        jax.ShapeDtypeStruct((4, 128, 128), F32),
        jax.ShapeDtypeStruct((4, 128, 128), F32),
    )
    shapes = lambda *dims, kind=F32: pltpu.VMEM(dims, kind)
    half = functools.partial(shapes, kind=BF16)
    gx, g1, g2 = pl.pallas_call(
        kernel,
        name="ffn_backward",
        out_shape=results,
        in_specs=[hbm] * 6,
        out_specs=(hbm,) * 3,
        scratch_shapes=[
            shapes(65, 128, 128), shapes(65, 128, 128),
            shapes(16, 256, 256), shapes(16, 256, 256),
            half(16, 256, 512), half(16, 256, 512),
            half(512, 256), half(512, 256), half(2, 512, 256), half(2, 512, 256),
            shapes(129, 128, 128),
            half(256, 256), half(256, 256),
            shapes(256, 512), shapes(256, 512), shapes(256, 512),
            half(512, 256), half(512, 256), half(512, 256), half(512, 256),
            half(256, 512), half(256, 512),
            shapes(16, 256, 256), shapes(30, 128, 256),
            shapes(2, 2, 16, 128, 128), shapes(2, 2, 2, 6, 128, 128), shapes(2, 4, 128, 128),
            shapes(2, 128, kind=jnp.int32), pltpu.SMEM((2, 128), jnp.int32), pltpu.SMEM((16,), jnp.int32),
            pltpu.SMEM((4, 16), jnp.int32), pltpu.SMEM((4, 16), jnp.int32),
            pltpu.SMEM((64,), jnp.int32), pltpu.SMEM((64,), jnp.int32),
            pltpu.SemaphoreType.DMA((9,)),
            pltpu.SemaphoreType.DMA((N_COPIES,)),
            pltpu.SemaphoreType.DMA((10,)),
        ],
        compiler_params=pltpu.CompilerParams(
            collective_id=0, has_side_effects=True, vmem_limit_bytes=60_000_000
        ),
    )(ids(slots_one), ids(slots_two), inputs, grad_out, w1, w2)
    factor = 1.0 / math.sqrt(inputs.shape[0] * lax.axis_size("tok"))
    gx, g1, g2 = pl.pallas_call(
        functools.partial(finish, factor),
        name="ffn_finish",
        out_shape=results,
        in_specs=[vmem] * 3,
        out_specs=(vmem,) * 3,
    )(gx, g1, g2)
    return gx, g1.reshape(1, 1, 4, 128, 128), g2.reshape(1, 1, 4, 128, 128)


def solution(mesh):
    in_specs = (
        P("tok", "ch"),
        P("tok", "ch"),
        P(None, "ch", None, None, None),
        P(None, "ch", None),
        P(None, "ch", None, None, None),
        P(None, "ch", None),
    )
    out_specs = (P("tok", "ch"), P("tok", "ch", None, None, None), P("tok", "ch", None, None, None))
    return jax.shard_map(body, mesh=mesh, in_specs=in_specs, out_specs=out_specs, check_vma=False)
```

```python
import functools
import math

import jax
import jax.numpy as jnp
from jax import lax
from jax.experimental import pallas as pl
from jax.experimental.pallas import tpu as pltpu
from jax.sharding import PartitionSpec as P

F32 = jnp.float32
BF16 = jnp.bfloat16
MESH = pl.DeviceIdType.MESH
NZ, NXL, NXH, NY = 8, 2, 2, 4

SLOTS = [
    (0, 0),
    (0, -1), (0, 1), (1, 0),
    (0, -2), (0, 2), (1, 1),
    (0, -3), (0, 3), (1, -1),
    (0, 4), (1, -2), (1, 2),
    (1, -3), (1, 3), (1, 4),
]
SLOT = {key: at for at, key in enumerate(SLOTS)}
SLOT[(0, -4)] = SLOT[(0, 4)]
SLOT[(1, -4)] = SLOT[(1, 4)]
NT = (((1,), (1,)), ((), ()))
NN = (((1,), (0,)), ((), ()))

N_COPIES = 60 + 30 + 30


def dot(a, b, dims):
    return lax.dot_general(a, b, dims, preferred_element_type=F32)


def split(v):
    high = v.astype(BF16)
    return high, (v - high.astype(F32)).astype(BF16)


def kernel(
    ids1_in, ids2_in, x_in, dy_in, w1_hbm, w2_hbm,
    gx_out, g1_out, g2_out,
    raw1, raw2, xg, dyg, w1h, w1l, w2h, w2l, last_h, last_l, table,
    sh, sl, pre, ga, slope, act_th, act_tl, gp_th, gp_tl, gph, gpl,
    gx, rs_buf, core_buf, y_buf, far_buf, fill_v, fill, slot_of, ids1, ids2, where1, where2,
    send_sem, recv_sem, local_sem,
):
    t = lax.axis_index("tok")
    c = lax.axis_index("ch")
    core = lax.rem(t, 2)
    y = lax.rem(lax.div(t, 2), NY)
    xh = lax.div(t, 2 * NY)
    xl = lax.rem(c, 2)
    z = lax.div(c, 2)

    def at_z(step):
        return (t, lax.rem(z + step, NZ) * 2 + xl)

    def at_y(step):
        return ((xh * NY + lax.rem(y + step, NY)) * 2 + core, c)

    zp, zm = at_z(1), at_z(NZ - 1)
    yp, ym = at_y(1), at_y(NY - 1)
    xp = (t, z * 2 + (1 - xl))
    cp = ((xh * NY + y) * 2 + (1 - core), c)
    hp = (((1 - xh) * NY + y) * 2 + core, c)

    fetches = [
        pltpu.make_async_copy(src, dst, local_sem.at[at])
        for at, (src, dst) in enumerate(
            (
                (ids1_in, ids1),
                (ids2_in, ids2),
                (x_in, xg.at[0]),
                (w1_hbm, raw1.at[pl.ds(0, 64)]),
                (dy_in, dyg.at[0]),
                (w2_hbm, raw2.at[pl.ds(0, 64)]),
            )
        )
    ]

    barrier = pltpu.get_barrier_semaphore()
    for peer in (zp, zm, xp, yp, ym, cp, hp):
        pl.semaphore_signal(barrier, inc=1, device_id=peer, device_id_type=MESH)
    for fetch in fetches:
        fetch.start()
    pl.semaphore_wait(barrier, 7)

    copies = []
    sent = {
        0: xg.at[pl.ds(0, 15)], 1: dyg.at[pl.ds(0, 15)], 2: rs_buf,
        3: core_buf.at[0], 4: core_buf.at[1], 5: y_buf.at[0], 6: y_buf.at[1],
        7: far_buf.at[0], 8: far_buf.at[1],
    }

    def all_sent(group):
        whole = sent[group]
        pltpu.make_async_remote_copy(
            src_ref=whole, dst_ref=whole, send_sem=send_sem.at[group], recv_sem=recv_sem.at[0],
            device_id=zp, device_id_type=MESH,
        ).wait_send()


    def send(src, dst, peer, group):
        at = len(copies)
        copy = pltpu.make_async_remote_copy(
            src_ref=src, dst_ref=dst, send_sem=send_sem.at[group], recv_sem=recv_sem.at[at],
            device_id=peer, device_id_type=MESH,
        )
        copy.start()
        copies.append(copy)
        return copy

    rows = {"a": pl.ds(0, 128), "b": pl.ds(128, 128)}
    arrivals = {}

    def forward(phase, source, col, dz, half, link):
        peer = {"+": zp, "-": zm, "x": xp}[link]
        to = {"+": (col, dz - 1), "-": (col, dz + 1), "x": (1 - col, dz)}[link]
        buf = xg if phase == 0 else dyg
        src = source if (col, dz) == (0, 0) else buf.at[SLOT[(col, dz)]]
        copy = send(src.at[rows[half]], buf.at[SLOT[to], rows[half]], peer, phase)
        arrivals[(phase, SLOT[to], half)] = copy

    def arrive(phase, key, halves="ab"):
        for half in halves:
            arrivals[(phase, SLOT[key], half)].wait_recv()

    def open_phase(phase, source):
        for one, two in ("ab", "ba"):
            forward(phase, source, 0, 0, one, "+")
            forward(phase, source, 0, 0, two, "-")
            forward(phase, source, 0, 0, one, "x")

    def gather(phase, source, take, take_last, then):
        def hand_on(col, dz, half, links):
            arrive(phase, (col, dz), half)
            for link in links:
                forward(phase, source, col, dz, half, link)

        for one, two in ("ab", "ba"):
            hand_on(0, -1, one, "+")
            hand_on(0, 1, two, "-x")
        forward(phase, source, 0, -1, "a", "x")
        forward(phase, source, 0, -1, "b", "x")
        run(take, 1, 3)
        arrive(phase, (1, 0))
        run(take, 3, 4)
        for one, two in ("ab", "ba"):
            hand_on(0, -2, one, "+")
            hand_on(0, 2, two, "-")
        run(take, 4, 6)
        arrive(phase, (1, 1))
        run(take, 6, 7)
        hand_on(0, -3, "a", "+x")
        hand_on(0, 3, "b", "-x")
        hand_on(0, -3, "b", "x")
        hand_on(0, 3, "a", "x")
        hand_on(1, -1, "a", "+")
        hand_on(1, -1, "b", "+")
        forward(phase, source, 1, 1, "b", "-")
        forward(phase, source, 1, 1, "a", "-")
        run(take, 7, 10)
        hand_on(1, -3, "a", "+")
        arrive(phase, (0, 4))
        run(take, 10, 11)
        hand_on(1, 3, "b", "-")
        then()
        arrive(phase, (1, -2))
        arrive(phase, (1, 2))
        run(take, 11, 13)
        arrive(phase, (1, -3), "b")
        run(take, 13, 14)
        arrive(phase, (1, 3), "a")
        arrive(phase, (1, 4))
        run(take_last, 14, 16)

    def take_x(s, carry):
        for q in range(2):
            for h in range(4):
                high, low = split(raw1[fill[0, s * 8 + q * 4 + h]])
                w1h[s, pl.ds(q * 128, 128), pl.ds(h * 128, 128)] = high
                w1l[s, pl.ds(q * 128, 128), pl.ds(h * 128, 128)] = low
        high, low = split(xg[s])
        sh[...] = high
        sl[...] = low
        pre[...] += (
            dot(sh[...], w1h[s], NN) + dot(sh[...], w1l[s], NN) + dot(sl[...], w1h[s], NN)
        )
        return carry

    def to_table(s, th, tl):
        full = dot(th[...], sh[...], NN) + dot(th[...], sl[...], NN) + dot(tl[...], sh[...], NN)
        for q in range(2):
            for h in range(4):
                table[s * 8 + q * 4 + h] = full[h * 128 : h * 128 + 128, q * 128 : q * 128 + 128]

    def load_dy(s):
        high, low = split(dyg[s])
        sh[...] = high
        sl[...] = low

    def fill_w2(s, to_h, to_l):
        for q in range(2):
            for h in range(4):
                high, low = split(raw2[fill[1, s * 8 + q * 4 + h]])
                to_h[pl.ds(h * 128, 128), pl.ds(q * 128, 128)] = high
                to_l[pl.ds(h * 128, 128), pl.ds(q * 128, 128)] = low

    def add_ga(wh, wl):
        ga[...] += dot(sh[...], wh[...], NT) + dot(sh[...], wl[...], NT) + dot(sl[...], wh[...], NT)

    def take_dy(s, carry):
        load_dy(s)
        fill_w2(s, w2h, w2l)
        add_ga(w2h, w2l)
        to_table(s, act_th, act_tl)
        return carry

    def fill_last(i, carry):
        fill_w2(14 + i, last_h.at[i], last_l.at[i])
        return carry

    def take_ga(s, carry):
        load_dy(s)
        add_ga(last_h.at[s - 14], last_l.at[s - 14])
        return carry

    def take_dw2(s, carry):
        load_dy(s)
        to_table(s, act_th, act_tl)
        return carry

    def take_w1(s, carry):
        high, low = split(xg[s])
        sh[...] = high
        sl[...] = low
        to_table(s, gp_th, gp_tl)
        return carry

    def grad_x(s, carry):
        gx[s] = dot(gph[...], w1h[s], NT) + dot(gph[...], w1l[s], NT) + dot(gpl[...], w1h[s], NT)
        return carry

    def run(body, first, last):
        lax.fori_loop(first, last, body, 0)

    def transposed(value, r, th, tl):
        high, low = split(value.T)
        th[:, r] = high
        tl[:, r] = low

    def lies(w, o, e):
        if w == 0:
            name = ids1[e, o]
            f, h = lax.div(name, 4), lax.rem(name, 4)
        else:
            name = ids2[e, o]
            f, h = lax.rem(name, 32), lax.div(name, 32)
        shard, q = lax.div(f, 2), lax.rem(f, 2)
        dz = lax.rem(lax.div(shard, 2) + (NZ - z), NZ)
        xs = lax.rem(shard, 2)
        slot = slot_of[(xs + xl - 2 * xs * xl) * NZ + dz]
        return jnp.where(name < 128, slot * 8 + q * 4 + h, 128)

    def fill_tables():
        lane = lax.broadcasted_iota(jnp.int32, (1, 128), 1)
        place = lax.div(lane, 8)
        shard = jnp.zeros_like(lane)
        for s, (col, dz) in enumerate(SLOTS):
            its = lax.rem(z + (dz + NZ), NZ) * 2 + xl + col - 2 * xl * col
            shard = jnp.where(place == s, its, shard)
            slot_of[col * NZ + (dz + NZ) % NZ] = jnp.int32(s)
        f = shard * 2 + lax.rem(lax.div(lane, 4), 2)
        h = lax.rem(lane, 4)
        one, two = f * 4 + h, h * 32 + f

        def owner(o, carry):
            a, b = carry
            for e in range(4):
                entry = o * 4 + e
                a = jnp.where(one == ids1[e, o], entry, a)
                b = jnp.where(two == ids2[e, o], entry, b)
            return a, b

        empty = jnp.full((1, 128), 64, jnp.int32)
        a, b = lax.fori_loop(0, 16, owner, (empty, empty))
        fill_v[0:1, :] = a
        fill_v[1:2, :] = b
        to_smem = pltpu.make_async_copy(fill_v, fill, local_sem.at[6])
        to_smem.start()
        to_smem.wait()

    def find_entries():
        def owner(o, carry):
            for e in range(4):
                where1[o * 4 + e] = lies(0, o, e)
                where2[o * 4 + e] = lies(1, o, e)
            return carry

        lax.fori_loop(0, 16, owner, 0)

    open_phase(0, x_in)
    fetches[0].wait()
    fetches[1].wait()
    fill_tables()
    pre[...] = jnp.zeros_like(pre)
    ga[...] = jnp.zeros_like(ga)
    zero = jnp.zeros((128, 128), F32)
    raw1[64] = zero
    raw2[64] = zero
    table[128] = zero
    for fetch in fetches[2:]:
        fetch.wait()
    run(take_x, 0, 1)

    def next_phase():
        open_phase(1, dy_in)
        find_entries()

    gather(0, x_in, take_x, take_x, next_phase)
    for part in range(2):
        r = pl.ds(part * 128, 128)
        p = pre[r, :]
        cdf = 0.5 * (1.0 + lax.erf(p * (1.0 / math.sqrt(2.0))))
        pdf = jnp.exp(-0.5 * p * p) * (1.0 / math.sqrt(2.0 * math.pi))
        slope[r, :] = cdf + p * pdf
        transposed(p * cdf, r, act_th, act_tl)
    run(take_dy, 0, 1)
    gather(1, dy_in, take_dy, take_dw2, lambda: run(fill_last, 0, 2))

    def pack(w, raw, rxh, first, last):
        where = where2 if w else where1

        def one(i, carry):
            rc = lax.rem(i, 2)
            ry = lax.div(i, 2)
            owner_y = lax.rem(y + ry, NY)
            owner_x = xh + rxh - 2 * xh * rxh
            owner_c = core + rc - 2 * core * rc
            owner = (owner_x * NY + owner_y) * 2 + owner_c
            for e in range(4):
                raw[((rc * 2 + rxh) * NY + ry) * 4 + e] = table[where[owner * 4 + e]]
            return carry

        lax.fori_loop(2 * first, 2 * last, one, 0)

    def mine(raw, rxh, ry, first, count):
        return raw.at[pl.ds((rxh * NY + ry) * 4 + first, count)]

    def swap_cores(w, raw, rxh, first, last):
        r = pl.ds(first * 4, (last - first) * 4)
        theirs = pl.ds(((2 + rxh) * NY + first) * 4, (last - first) * 4)
        return send(raw.at[theirs], core_buf.at[w, rxh, r], cp, 3 + w), first, last

    def add_core(swap, w, raw, rxh):
        copy, first, last = swap
        copy.wait_recv()
        ours = pl.ds((rxh * NY + first) * 4, (last - first) * 4)
        raw[ours] = raw[ours] + core_buf[w, rxh, pl.ds(first * 4, (last - first) * 4)]

    def swap_all(w, raw):
        swaps = {}
        for rxh, first, last in ((1, 2, 3), (0, 2, 3), (1, 3, 4), (1, 0, 2), (0, 3, 4), (0, 0, 2)):
            pack(w, raw, rxh, first, last)
            swaps[(rxh, first)] = swap_cores(w, raw, rxh, first, last)
        return swaps

    def y_far(w, raw, rxh):
        return (
            send(mine(raw, rxh, 2, 0, 2), y_buf.at[w, rxh, 0, pl.ds(0, 2)], yp, 5 + w),
            send(mine(raw, rxh, 2, 2, 2), y_buf.at[w, rxh, 1, pl.ds(0, 2)], ym, 5 + w),
        )

    def y_near(pair, w, raw, rxh):
        at = (rxh * NY + 1) * 4
        pair[0].wait_recv()
        raw[pl.ds(at, 2)] = raw[pl.ds(at, 2)] + y_buf[w, rxh, 0, pl.ds(0, 2)]
        one = send(mine(raw, rxh, 1, 0, 4), y_buf.at[w, rxh, 0, pl.ds(2, 4)], yp, 5 + w)
        at = (rxh * NY + 3) * 4 + 2
        pair[1].wait_recv()
        raw[pl.ds(at, 2)] = raw[pl.ds(at, 2)] + y_buf[w, rxh, 1, pl.ds(0, 2)]
        two = send(mine(raw, rxh, 3, 0, 4), y_buf.at[w, rxh, 1, pl.ds(2, 4)], ym, 5 + w)
        return one, two

    def y_home(pair, w, raw, rxh):
        at = rxh * NY * 4
        pair[0].wait_recv()
        pair[1].wait_recv()
        raw[pl.ds(at, 4)] = (
            raw[pl.ds(at, 4)] + y_buf[w, rxh, 0, pl.ds(2, 4)] + y_buf[w, rxh, 1, pl.ds(2, 4)]
        )

    def far(w, raw):
        return send(mine(raw, 1, 0, 0, 4), far_buf.at[w], hp, 7 + w)

    inbound = {}

    def rs_send(col, dz, half, link):
        peer = {"+": zp, "-": zm, "x": xp}[link]
        to = {"+": (col, dz - 1), "-": (col, dz + 1), "x": (1 - col, dz)}[link]
        at = len(inbound)
        copy = send(gx.at[SLOT[(col, dz)], rows[half]], rs_buf.at[at], peer, 2)
        inbound[(col, dz, half)] = (copy, at, SLOT[to])

    def rs_add(col, dz, half):
        copy, at, slot = inbound[(col, dz, half)]
        copy.wait_recv()
        gx[slot, rows[half]] = gx[slot, rows[half]] + rs_buf[at]

    swap_2 = swap_all(1, raw2)
    run(take_ga, 14, 16)
    for part in range(2):
        r = pl.ds(part * 128, 128)
        grad_pre = ga[r, :] * slope[r, :]
        high, low = split(grad_pre)
        gph[r, :] = high
        gpl[r, :] = low
        transposed(grad_pre, r, gp_th, gp_tl)
    run(grad_x, 15, 16)
    rs_send(1, 4, "a", "x")
    rs_send(1, 4, "b", "x")
    add_core(swap_2[(1, 2)], 1, raw2, 1)
    far_21 = y_far(1, raw2, 1)
    run(grad_x, 13, 15)
    rs_send(1, 3, "b", "+")
    rs_send(1, -3, "a", "-")
    rs_send(1, 3, "a", "+")
    rs_send(1, -3, "b", "-")
    run(take_w1, 0, 3)
    add_core(swap_2[(0, 2)], 1, raw2, 0)
    far_20 = y_far(1, raw2, 0)
    run(take_w1, 3, 5)
    run(grad_x, 3, 4)
    rs_send(1, 0, "a", "x")
    rs_send(1, 0, "b", "x")
    add_core(swap_2[(1, 3)], 1, raw2, 1)
    add_core(swap_2[(1, 0)], 1, raw2, 1)
    add_core(swap_2[(0, 3)], 1, raw2, 0)
    add_core(swap_2[(0, 0)], 1, raw2, 0)
    run(grad_x, 11, 13)
    run(take_w1, 5, 8)
    near_21 = y_near(far_21, 1, raw2, 1)
    rs_add(1, 3, "b")
    rs_send(1, 2, "b", "+")
    rs_add(1, -3, "a")
    rs_send(1, -2, "a", "-")
    run(take_w1, 8, 16)
    swap_1 = swap_all(0, raw1)
    rs_add(1, 3, "a")
    rs_send(1, 2, "a", "+")
    rs_add(1, -3, "b")
    rs_send(1, -2, "b", "-")
    run(grad_x, 10, 11)
    rs_add(1, 4, "a")
    rs_send(0, 4, "a", "+")
    rs_add(1, 4, "b")
    rs_send(0, -4, "b", "-")
    add_core(swap_1[(1, 2)], 0, raw1, 1)
    far_11 = y_far(0, raw1, 1)
    run(grad_x, 6, 10)
    rs_send(0, 3, "b", "+")
    rs_send(0, -3, "a", "-")
    rs_add(1, 2, "b")
    rs_send(1, 1, "b", "x")
    rs_add(1, -2, "a")
    rs_send(1, -1, "a", "x")
    add_core(swap_1[(0, 2)], 0, raw1, 0)
    far_10 = y_far(0, raw1, 0)
    y_home(near_21, 1, raw2, 1)
    rs_add(1, 2, "a")
    rs_send(1, 1, "a", "x")
    rs_add(1, -2, "b")
    rs_send(1, -1, "b", "x")
    far_2 = far(1, raw2)
    add_core(swap_1[(1, 3)], 0, raw1, 1)
    add_core(swap_1[(1, 0)], 0, raw1, 1)
    add_core(swap_1[(0, 3)], 0, raw1, 0)
    add_core(swap_1[(0, 0)], 0, raw1, 0)
    run(grad_x, 0, 3)
    near_11 = y_near(far_11, 0, raw1, 1)
    run(grad_x, 4, 6)
    rs_add(0, 4, "a")
    rs_send(0, 3, "a", "+")
    rs_add(0, -4, "b")
    rs_send(0, -3, "b", "-")
    rs_add(1, 0, "a")
    rs_add(1, 0, "b")
    all_sent(0)
    all_sent(1)
    rs_add(0, 3, "b")
    rs_send(0, 2, "b", "+")
    rs_add(0, -3, "a")
    rs_send(0, -2, "a", "-")
    rs_add(0, 3, "a")
    rs_send(0, 2, "a", "+")
    rs_add(0, -3, "b")
    rs_send(0, -2, "b", "-")
    near_20 = y_near(far_20, 1, raw2, 0)
    y_home(near_11, 0, raw1, 1)
    far_1 = far(0, raw1)
    near_10 = y_near(far_10, 0, raw1, 0)
    rs_add(1, 1, "b")
    rs_add(0, 2, "b")
    rs_send(0, 1, "b", "+")
    rs_add(1, -1, "a")
    rs_add(0, -2, "a")
    rs_send(0, -1, "a", "-")
    rs_add(1, 1, "a")
    rs_add(0, 2, "a")
    rs_send(0, 1, "a", "+")
    rs_add(1, -1, "b")
    rs_add(0, -2, "b")
    rs_send(0, -1, "b", "-")
    y_home(near_20, 1, raw2, 0)
    far_2.wait_recv()
    raw2[pl.ds(0, 4)] = raw2[pl.ds(0, 4)] + far_buf[1]
    put_g2 = pltpu.make_async_copy(raw2.at[pl.ds(0, 4)], g2_out, local_sem.at[7])
    put_g2.start()
    rs_add(0, 1, "b")
    rs_add(0, -1, "a")
    rs_add(0, 1, "a")
    rs_add(0, -1, "b")
    put_gx = pltpu.make_async_copy(gx.at[0], gx_out, local_sem.at[8])
    put_gx.start()
    y_home(near_10, 0, raw1, 0)
    far_1.wait_recv()
    raw1[pl.ds(0, 4)] = raw1[pl.ds(0, 4)] + far_buf[0]
    put_g1 = pltpu.make_async_copy(raw1.at[pl.ds(0, 4)], g1_out, local_sem.at[9])
    put_g1.start()
    for group in range(2, 9):
        all_sent(group)
    put_g2.wait()
    put_gx.wait()
    put_g1.wait()
    assert len(copies) == N_COPIES


def finish(factor, gx_in, g1_in, g2_in, gx_out, g1_out, g2_out):
    gx_out[...] = gx_in[...]
    for e in range(4):
        g1_out[e] = g1_in[e].T * factor
        g2_out[e] = g2_in[e] * factor


def body(inputs, grad_out, blocks_one, slots_one, blocks_two, slots_two):
    w1 = blocks_one.reshape(64, 128, 128)
    w2 = blocks_two.reshape(64, 128, 128)
    vmem = pl.BlockSpec(memory_space=pltpu.VMEM)
    hbm = pl.BlockSpec(memory_space=pltpu.HBM)
    ids = lambda slots: slots.transpose(1, 2, 0).reshape(4, 16)
    results = (
        jax.ShapeDtypeStruct((256, 256), F32),
        jax.ShapeDtypeStruct((4, 128, 128), F32),
        jax.ShapeDtypeStruct((4, 128, 128), F32),
    )
    shapes = lambda *dims, kind=F32: pltpu.VMEM(dims, kind)
    half = functools.partial(shapes, kind=BF16)
    gx, g1, g2 = pl.pallas_call(
        kernel,
        name="ffn_backward",
        out_shape=results,
        in_specs=[hbm] * 6,
        out_specs=(hbm,) * 3,
        scratch_shapes=[
            shapes(65, 128, 128), shapes(65, 128, 128),
            shapes(16, 256, 256), shapes(16, 256, 256),
            half(16, 256, 512), half(16, 256, 512),
            half(512, 256), half(512, 256), half(2, 512, 256), half(2, 512, 256),
            shapes(129, 128, 128),
            half(256, 256), half(256, 256),
            shapes(256, 512), shapes(256, 512), shapes(256, 512),
            half(512, 256), half(512, 256), half(512, 256), half(512, 256),
            half(256, 512), half(256, 512),
            shapes(16, 256, 256), shapes(30, 128, 256),
            shapes(2, 2, 16, 128, 128), shapes(2, 2, 2, 6, 128, 128), shapes(2, 4, 128, 128),
            shapes(2, 128, kind=jnp.int32), pltpu.SMEM((2, 128), jnp.int32), pltpu.SMEM((16,), jnp.int32),
            pltpu.SMEM((4, 16), jnp.int32), pltpu.SMEM((4, 16), jnp.int32),
            pltpu.SMEM((64,), jnp.int32), pltpu.SMEM((64,), jnp.int32),
            pltpu.SemaphoreType.DMA((9,)),
            pltpu.SemaphoreType.DMA((N_COPIES,)),
            pltpu.SemaphoreType.DMA((10,)),
        ],
        compiler_params=pltpu.CompilerParams(
            collective_id=0, has_side_effects=True, vmem_limit_bytes=60_000_000
        ),
    )(ids(slots_one), ids(slots_two), inputs, grad_out, w1, w2)
    factor = 1.0 / math.sqrt(inputs.shape[0] * lax.axis_size("tok"))
    gx, g1, g2 = pl.pallas_call(
        functools.partial(finish, factor),
        name="ffn_finish",
        out_shape=results,
        in_specs=[vmem] * 3,
        out_specs=(vmem,) * 3,
    )(gx, g1, g2)
    return gx, g1.reshape(1, 1, 4, 128, 128), g2.reshape(1, 1, 4, 128, 128)


def solution(mesh):
    in_specs = (
        P("tok", "ch"),
        P("tok", "ch"),
        P(None, "ch", None, None, None),
        P(None, "ch", None),
        P(None, "ch", None, None, None),
        P(None, "ch", None),
    )
    out_specs = (P("tok", "ch"), P("tok", "ch", None, None, None), P("tok", "ch", None, None, None))
    return jax.shard_map(body, mesh=mesh, in_specs=in_specs, out_specs=out_specs, check_vma=False)
```
